32 devices in a mesh: space: 8 (over y, x, core), tm: 4 (over z).
Axes of the slice: x: 2, y: 2, z: 4, core: 2. Of those that a mesh axis runs over, the one named last changes fastest.
Arguments:
- series: bfloat16 [16384, 2, 512], P('space', None, 'tm'), may hold values from -6 to 6
- space_basis: bfloat16 [16384, 16384], P('space', 'tm'), may hold values from -0.046875 to 0.046875
- time_basis: bfloat16 [512, 512], P('tm'), may hold values from -0.25 to 0.25
- space_eig: float32 [16384], replicated, may hold values from 0.3 to 3
- time_eig: float32 [512], replicated, may hold values from 0.3 to 3
Outputs:
- alpha: bfloat16 [16384, 2, 512], P('space', None, 'tm')
- grad_space: bfloat16 [16384, 8, 2048], P('space', None, 'tm')
The draws below stay inside these ranges and needn't reach their ends.
All inputs are finite; a program needn't handle non-finite values.
Results may differ from the reference program's by a relative error of at most 0.0063.
Values may be sent and summed in bfloat16 or wider, within the bound.
A program may use at most 128 MiB of HBM per device.

```python
import math
import jax
import jax.numpy as jnp

STATIONS = 16384
TIMES = 512
REPS = 2
N_SPACE = 8


def steps_of(stream_key, shape, cuts, smallest, high):
    level, own = 1.0, jax.random.fold_in(stream_key, 6)
    for dim, blocks in cuts:
        heights = jnp.exp(jax.random.uniform(jax.random.fold_in(own, dim), (blocks,), jnp.float32, smallest / len(cuts), high / len(cuts)))
        level = level * jnp.repeat(heights, shape[dim] // blocks).reshape([-1 if axis == dim else 1 for axis in range(len(shape))])
    return level


def bell_draw(stream_key, extent, spread, reach, split=(), held_as=jnp.bfloat16):
    entries = jax.random.normal(stream_key, extent, jnp.float32) * spread
    if len(split) > 0:
        entries = steps_of(stream_key, extent, split, -0.22, 0.18) * entries
    return jnp.clip(entries, min=-reach, max=reach).astype(held_as)


def setup_inputs(seed: int = 0) -> dict:
    splits = jax.random.split(jax.random.key(seed), 6)
    return {
        "series": bell_draw(splits[0], (STATIONS, REPS, TIMES), 1.0, 6.0, ((0, 8), (2, 4))),
        "space_basis": bell_draw(splits[1], (STATIONS, STATIONS), STATIONS ** -0.5, 0.046875, ((0, 8), (1, 4))),
        "time_basis": bell_draw(splits[2], (TIMES, TIMES), TIMES ** -0.5, 0.25, ((0, 4),)),
        "space_eig": jnp.clip(jnp.exp(jax.random.uniform(splits[3], (STATIONS,), jnp.float32, math.log(0.3), math.log(3.0))), 0.3, 3.0),
        "time_eig": jnp.clip(jnp.exp(jax.random.uniform(splits[4], (TIMES,), jnp.float32, math.log(0.3), math.log(3.0))), 0.3, 3.0),
    }


def reference(series, space_basis, time_basis, space_eig, time_eig):
    flat = series.reshape(STATIONS * REPS, TIMES)
    rotated = jnp.dot(flat, time_basis, preferred_element_type=jnp.float32).astype(jnp.bfloat16)
    rotated = rotated.reshape(STATIONS, REPS * TIMES)
    spectral = jnp.dot(space_basis.T, rotated, preferred_element_type=jnp.float32)
    denom = space_eig[:, None, None] * time_eig[None, None, :] + 0.1
    scaled_spec = (spectral.reshape(STATIONS, REPS, TIMES) / denom).astype(jnp.bfloat16)
    scaled_spec = scaled_spec.reshape(STATIONS, REPS * TIMES)
    back = jnp.dot(space_basis, scaled_spec, preferred_element_type=jnp.float32).astype(jnp.bfloat16)
    alpha = jnp.dot(back.reshape(STATIONS * REPS, TIMES), time_basis.T, preferred_element_type=jnp.float32)
    alpha = alpha.astype(jnp.bfloat16).reshape(STATIONS, REPS, TIMES)
    weighted = back.reshape(STATIONS, REPS, TIMES).astype(jnp.float32) * time_eig[None, None, :]
    weighted = (weighted / (REPS * TIMES)).astype(jnp.bfloat16).reshape(STATIONS, REPS * TIMES)
    grad = jnp.dot(weighted, back.T, preferred_element_type=jnp.float32).astype(jnp.bfloat16)
    return alpha, grad.reshape(STATIONS, N_SPACE, STATIONS // N_SPACE)
```

```python
import functools

import jax
import jax.numpy as jnp
from jax import lax
from jax.experimental import pallas as pl
from jax.experimental.pallas import tpu as pltpu
from jax.sharding import PartitionSpec as P

F32 = jnp.float32
BF16 = jnp.bfloat16
MESH = pl.DeviceIdType.MESH
CONTRACT_LAST = (((1,), (1,)), ((), ()))
CONTRACT_FIRST = (((0,), (0,)), ((), ()))
VMEM_BYTES = 67043328
RING = 4
PIECES = 2


def rcopy(src, dst, send_sem, recv_sem, **where):
    return pltpu.make_async_remote_copy(
        src_ref=src,
        dst_ref=dst,
        send_sem=send_sem,
        recv_sem=recv_sem,
        device_id=where,
        device_id_type=MESH,
    )


def field_kernel(
    space_count,
    time_count,
    series_hbm, basis_hbm, tbasis_hbm, time_eig_ref, space_eig_ref,
    rows_hbm, cols_hbm,
    basis, series, tbasis, pair_out, pair_in, chip_out, chip_in, mine, scaled, partial, below, above, up_out, down_out,
    load_sem, xs_sem, xr_sem, ts_sem, tr_sem, ps_sem, pr_sem, cs_sem, cr_sem, gs_sem, gr_sem, fs_sem,
    us_sem, ur_sem, ds_sem, dr_sem, os_sem, ks_sem, kr_sem, kf_sem, ko_sem,
):
    reps, _, time_local, _ = series.shape
    _, blocks, block_rows, times = partial.shape
    own = mine.shape[1]
    pairs = space_count // 2
    last = time_count - 1
    sub_rows = blocks * block_rows // time_count
    me = lax.axis_index("space")
    z = lax.axis_index("tm")
    core = lax.rem(me, 2)
    chip = lax.div(me, 2)
    partner = me + 1 - 2 * core
    total = reps * blocks

    def chip_at(d):
        return lax.bitwise_xor(chip, d)

    def peer(d):
        return 2 * chip_at(d) + core

    barrier = pltpu.get_barrier_semaphore()

    def greet(**where):
        pl.semaphore_signal(barrier, inc=1, device_id=where, device_id_type=MESH)

    @pl.when(z > 0)
    def _():
        greet(tm=z - 1)

    @pl.when(z < last)
    def _():
        greet(tm=z + 1)

    greet(space=partner)
    for d in range(1, pairs):
        greet(space=peer(d))

    load_basis = pltpu.make_async_copy(basis_hbm, basis, load_sem.at[0])
    load_basis.start()
    load_tbasis = pltpu.make_async_copy(tbasis_hbm, tbasis.at[z], load_sem.at[1])
    load_tbasis.start()
    loads = [pltpu.make_async_copy(series_hbm.at[q], series.at[q, z], load_sem.at[2 + q]) for q in range(reps)]
    for load in loads:
        load.start()

    @pl.when(z == 0)
    def _():
        below[...] = jnp.zeros_like(below)

    @pl.when(z == last)
    def _():
        above[...] = jnp.zeros_like(above)

    pl.semaphore_wait(barrier, pairs + jnp.minimum(z, 1) + jnp.minimum(last - z, 1))

    def x_copy(q, j, way, step):
        return rcopy(series.at[q, j], series.at[q, j], xs_sem.at[q, way, step], xr_sem.at[q, j], tm=z + 1 - 2 * way)

    def t_copy(j, way, step):
        return rcopy(tbasis.at[j], tbasis.at[j], ts_sem.at[way, step], tr_sem.at[j], tm=z + 1 - 2 * way)

    def line_start(copy):
        @pl.when(z < last)
        def _():
            copy(z, 0, 0).start()

        @pl.when(z > 0)
        def _():
            copy(z, 1, 0).start()

    def line_step(copy, k):
        @pl.when(z >= k)
        def _():
            copy(z - k, 0, k).wait_recv()

            @pl.when(z < last)
            def _():
                copy(z - k, 0, k).start()

        @pl.when(z + k <= last)
        def _():
            copy(z + k, 1, k).wait_recv()

            @pl.when(z > 0)
            def _():
                copy(z + k, 1, k).start()

    def line_drain(copy):
        for k in range(time_count):
            @pl.when((z >= k) & (z < last))
            def _():
                copy(z - k, 0, k).wait_send()

            @pl.when((z + k <= last) & (z > 0))
            def _():
                copy(z + k, 1, k).wait_send()

    def x_of(q):
        return functools.partial(x_copy, q)

    def pair_copy(q, d):
        return rcopy(pair_out.at[d], pair_in.at[q, d], ps_sem.at[d], pr_sem.at[q, d], space=partner)

    def chip_copy(q, d):
        return rcopy(chip_out.at[d - 1], chip_in.at[q, d - 1], cs_sem.at[d - 1], cr_sem.at[q, d - 1], space=peer(d))

    def spectrum(q, j):
        flat = series[q].reshape(time_count * time_local, series.shape[3])
        return jnp.dot(flat, basis[:, pl.ds(pl.multiple_of(j * own, own), own)], preferred_element_type=F32)

    def spectral_pair(q):
        @pl.loop(0, pairs)
        def _(n):
            d = pairs - 1 - n
            if q > 0:
                pair_copy(q - 1, d).wait_send()
            pair_out[d] = spectrum(q, 2 * chip_at(d) + 1 - core).astype(BF16)
            pair_copy(q, d).start()

    def spectral_own(q):
        @pl.loop(0, pairs)
        def _(n):
            d = pairs - 1 - n
            value = spectrum(q, peer(d))
            pair_copy(q, d).wait_recv()
            value = value + pair_in[q, d].astype(F32)

            @pl.when(d > 0)
            def _():
                if q > 0:
                    chip_copy(q - 1, d).wait_send()
                chip_out[d - 1] = value.astype(BF16)
                chip_copy(q, d).start()

            @pl.when(d == 0)
            def _():
                mine[...] = value

    def gather_copy(q, d):
        at = pl.ds(pl.multiple_of(me * own, own), own)
        return rcopy(scaled.at[q, :, at], scaled.at[q, :, at], gs_sem.at[q, d - 1], gr_sem.at[q, me], space=peer(d))

    def forward_copy(q, j, d):
        at = pl.ds(pl.multiple_of(j * own, own), own)
        return rcopy(scaled.at[q, :, at], scaled.at[q, :, at], fs_sem.at[q, d], gr_sem.at[q, j], space=partner)

    def scale_own(q):
        value = mine[...]
        for d in range(1, pairs):
            chip_copy(q, d).wait_recv()
            value = value + chip_in[q, d - 1].astype(F32)
        rotation = tbasis[...].reshape(time_count * time_local, times)
        turned = lax.dot_general(rotation, value.astype(BF16), CONTRACT_FIRST, preferred_element_type=F32)
        turned = turned / (time_eig_ref[...] * space_eig_ref[...] + 0.1)
        scaled[q, :, pl.ds(pl.multiple_of(me * own, own), own)] = turned.astype(BF16)
        for d in reversed(range(1, pairs)):
            gather_copy(q, d).start()
        forward_copy(q, me, 0).start()

    def gather_forward(q):
        for d in range(1, pairs):
            forward_copy(q, peer(d), d).wait_recv()
            forward_copy(q, peer(d), d).start()

    def gather_finish(q):
        for d in range(pairs):
            forward_copy(q, peer(d) + 1 - 2 * core, d).wait_recv()

    def back(q, i):
        low = lax.div(i, 2)
        side = lax.rem(i, 2)
        side = jnp.where(2 * z < time_count, side, 1 - side)
        sub = jnp.where(side == 0, last - low, low)
        value = lax.dot_general(
            basis[pl.ds(pl.multiple_of(sub * sub_rows, sub_rows), sub_rows), :],
            scaled[q],
            CONTRACT_LAST,
            preferred_element_type=F32,
        )
        partial[q, pl.ds(sub * PIECES, PIECES)] = value.reshape(PIECES, block_rows, times)

    def up_copy(n, q, m):
        slot = lax.rem(n, RING)
        return rcopy(up_out.at[slot], below.at[q, m], us_sem.at[slot], ur_sem.at[n], tm=z + 1)

    def down_copy(n, q, m):
        slot = lax.rem(n, RING)
        return rcopy(down_out.at[slot], above.at[q, m], ds_sem.at[slot], dr_sem.at[n], tm=z - 1)

    def row_copy(q, m):
        return pltpu.make_async_copy(below.at[q, m], rows_hbm.at[q, m], os_sem.at[q * blocks + m])

    def finish_block(q, m):
        below[q, m] = (partial[q, m] + below[q, m].astype(F32) + above[q, m].astype(F32)).astype(BF16)
        row_copy(q, m).start()

    def up_step(n):
        at = n - z

        @pl.when((at >= 0) & (at < total))
        def _():
            q = lax.div(at, blocks)
            m = blocks - 1 - lax.rem(at, blocks)

            @pl.when(z > 0)
            def _():
                up_copy(at, q, m).wait_recv()

            @pl.when(z < last)
            def _():
                @pl.when(at >= RING)
                def _():
                    up_copy(at, q, m).wait_send()

                up_out[lax.rem(at, RING)] = (partial[q, m] + below[q, m].astype(F32)).astype(BF16)
                up_copy(at, q, m).start()

            @pl.when(q * blocks + m + last - z < n)
            def _():
                finish_block(q, m)

    def down_step(n):
        at = n - (last - z)

        @pl.when((at >= 0) & (at < total))
        def _():
            q = lax.div(at, blocks)
            m = lax.rem(at, blocks)

            @pl.when(z < last)
            def _():
                down_copy(at, q, m).wait_recv()

            @pl.when(z > 0)
            def _():
                @pl.when(at >= RING)
                def _():
                    down_copy(at, q, m).wait_send()

                down_out[lax.rem(at, RING)] = (partial[q, m] + above[q, m].astype(F32)).astype(BF16)
                down_copy(at, q, m).start()

            @pl.when(q * blocks + blocks - 1 - m + z <= n)
            def _():
                finish_block(q, m)

    def column_source(q):
        return below.at[q, pl.ds(z * PIECES, PIECES)]

    def column_copy(q, d):
        return rcopy(column_source(q), cols_hbm.at[q, me], ks_sem.at[q, d], kr_sem.at[q, me], space=peer(d))

    def column_pair(q):
        return rcopy(column_source(q), cols_hbm.at[q, me], kf_sem.at[q, 0], kr_sem.at[q, me], space=partner)

    def column_own(q):
        return pltpu.make_async_copy(column_source(q), cols_hbm.at[q, me], ko_sem.at[q])

    def column_forward(q, j, d):
        return rcopy(cols_hbm.at[q, j], cols_hbm.at[q, j], kf_sem.at[q, d], kr_sem.at[q, j], space=partner)

    def columns_start(q):
        for d in reversed(range(1, pairs)):
            column_copy(q, d).start()
        column_pair(q).start()
        column_own(q).start()

    def columns_relay(q):
        for d in range(1, pairs):
            column_forward(q, peer(d), d).wait_recv()
            column_forward(q, peer(d), d).start()

    def columns_finish(q):
        for d in range(pairs):
            column_forward(q, peer(d) + 1 - 2 * core, d).wait_recv()
        for d in range(1, pairs):
            column_copy(q, d).wait_send()
            column_forward(q, peer(d), d).wait_send()
        column_pair(q).wait_send()
        column_own(q).wait()

    for load in loads:
        load.wait()
    load_tbasis.wait()
    line_start(x_of(0))
    for k in range(1, time_count - 1):
        line_step(x_of(0), k)
    line_start(t_copy)
    for q in range(1, reps):
        line_start(x_of(q))
    for k in range(max(1, time_count - 1), time_count):
        line_step(x_of(0), k)
    line_step(t_copy, 1)
    load_basis.wait()
    for q in range(reps):
        if q > 0:
            for k in range(max(1, time_count - 1), time_count):
                line_step(x_of(q), k)
        spectral_pair(q)
        if q + 1 < reps:
            line_step(x_of(q + 1), 1)
        if q > 0:
            gather_forward(q - 1)
        spectral_own(q)
        if q + 1 < reps:
            for k in range(2, time_count - 1):
                line_step(x_of(q + 1), k)
            if q == 0:
                for k in range(2, time_count):
                    line_step(t_copy, k)
            scale_own(q)

    ahead = blocks // 2

    @pl.loop(0, total + last)
    def _(n):
        q = lax.div(n, blocks)
        i = lax.rem(n, blocks)

        @pl.when((q < reps) & (i < time_count))
        def _():
            @pl.when(i == 0)
            def _():
                @pl.when(q == reps - 1)
                def _():
                    gather_forward(reps - 1)

                gather_finish(q)

            back(q, i)

        up_step(n)
        down_step(n)
        for r in range(reps):
            low = z * PIECES
            ready = r * blocks + jnp.maximum(blocks - 1 - low + z, low + PIECES - 1 + last - z)

            @pl.when(n == ready)
            def _():
                columns_start(r)

        @pl.when(n == ahead)
        def _():
            scale_own(reps - 1)

        @pl.when(n == total - 1)
        def _():
            for r in range(reps - 1):
                columns_relay(r)

    columns_relay(reps - 1)
    for q in range(reps):
        columns_finish(q)
        line_drain(x_of(q))
        for d in range(1, pairs):
            gather_copy(q, d).wait_send()
        for d in range(pairs):
            forward_copy(q, peer(d), d).wait_send()
    line_drain(t_copy)
    for d in range(pairs):
        pair_copy(reps - 1, d).wait_send()
        if d > 0:
            chip_copy(reps - 1, d).wait_send()

    @pl.loop(0, total)
    def _(n):
        row_copy(lax.div(n, blocks), lax.rem(n, blocks)).wait()

    for n in range(total - min(RING, total), total):
        q, m = n // blocks, n % blocks

        @pl.when(z < last)
        def _():
            up_copy(n, q, m).wait_send()

        @pl.when(z > 0)
        def _():
            down_copy(n, q, m).wait_send()


def solve_field(series, basis, tbasis, time_eig, space_eig, space_count, time_count):
    reps, time_local, rows = series.shape
    depth = basis.shape[1]
    times = tbasis.shape[1]
    own = depth // space_count
    pairs = space_count // 2
    blocks = PIECES * time_count
    block_rows = rows // blocks
    dma = pltpu.SemaphoreType.DMA
    hbm = pl.BlockSpec(memory_space=pl.ANY)
    vmem = pl.BlockSpec(memory_space=pltpu.VMEM)
    return pl.pallas_call(
        functools.partial(field_kernel, space_count, time_count),
        out_shape=(
            jax.ShapeDtypeStruct((reps, blocks, block_rows, times), BF16),
            jax.ShapeDtypeStruct((reps, space_count, PIECES, block_rows, times), BF16),
        ),
        in_specs=[hbm, hbm, hbm, vmem, vmem],
        out_specs=(hbm, hbm),
        scratch_shapes=[
            pltpu.VMEM((rows, depth), BF16),
            pltpu.VMEM((reps, time_count, time_local, rows), BF16),
            pltpu.VMEM((time_count, time_local, times), BF16),
            pltpu.VMEM((pairs, times, own), BF16),
            pltpu.VMEM((reps, pairs, times, own), BF16),
            pltpu.VMEM((pairs - 1, times, own), BF16),
            pltpu.VMEM((reps, pairs - 1, times, own), BF16),
            pltpu.VMEM((times, own), F32),
            pltpu.VMEM((reps, times, depth), BF16),
            pltpu.VMEM((reps, blocks, block_rows, times), F32),
            pltpu.VMEM((reps, blocks, block_rows, times), BF16),
            pltpu.VMEM((reps, blocks, block_rows, times), BF16),
            pltpu.VMEM((RING, block_rows, times), BF16),
            pltpu.VMEM((RING, block_rows, times), BF16),
            dma((2 + reps,)),
            dma((reps, 2, time_count)),
            dma((reps, time_count)),
            dma((2, time_count)),
            dma((time_count,)),
            dma((pairs,)),
            dma((reps, pairs)),
            dma((pairs - 1,)),
            dma((reps, pairs - 1)),
            dma((reps, pairs - 1)),
            dma((reps, space_count)),
            dma((reps, pairs)),
            dma((RING,)),
            dma((reps * blocks,)),
            dma((RING,)),
            dma((reps * blocks,)),
            dma((reps * blocks,)),
            dma((reps, pairs)),
            dma((reps, space_count)),
            dma((reps, pairs)),
            dma((reps,)),
        ],
        compiler_params=pltpu.CompilerParams(
            collective_id=0, has_side_effects=True, vmem_limit_bytes=VMEM_BYTES
        ),
    )(series, basis, tbasis, time_eig, space_eig)


def grad_kernel(reps, scale, *refs):
    rows, columns = refs[:reps], refs[reps : 2 * reps]
    eig_ref, basis_ref, alpha_ref, grad_ref, alpha_scr, grad_scr, weighted_scr = refs[2 * reps :]
    tile, blocks, _ = grad_ref.shape
    for q in range(reps):
        block = rows[q][0]
        weighted_scr[q] = (block.astype(F32) * eig_ref[...] / scale).astype(BF16)
        alpha_scr[pl.ds(q, tile, stride=reps), :] = lax.dot_general(
            block, basis_ref[...], CONTRACT_LAST, preferred_element_type=F32
        )
    alpha_ref[...] = alpha_scr[...].astype(BF16).reshape(alpha_ref.shape)

    sub = columns[0].shape[2]
    @pl.loop(0, blocks)
    def _(a):
        total = None
        for q in range(reps):
            part = lax.dot_general(
                weighted_scr[q], columns[q][0, a], CONTRACT_LAST, preferred_element_type=F32
            )
            total = part if total is None else total + part
        for w in range(0, sub, 128):
            grad_scr[w // 128, pl.ds(a, tile, stride=blocks), :] = total[:, w : w + 128]
    for w in range(0, sub, 128):
        grad_ref[:, :, w : w + 128] = (
            grad_scr[w // 128].astype(BF16).reshape(tile, blocks, 128)
        )


def grad_and_alpha(rows, columns, time_eig, time_basis):
    reps, row_count, times = rows.shape
    _, blocks, sub, _ = columns.shape
    time_local = time_basis.shape[0]
    tile = min(row_count, 512)
    row_specs = [pl.BlockSpec((1, tile, times), lambda i, q=q: (q, i, 0)) for q in range(reps)]
    col_specs = [pl.BlockSpec((1, blocks, sub, times), lambda i, q=q: (q, 0, 0, 0)) for q in range(reps)]
    return pl.pallas_call(
        lambda *refs: grad_kernel(reps, reps * times, *refs),
        out_shape=(
            jax.ShapeDtypeStruct((row_count, reps, time_local), BF16),
            jax.ShapeDtypeStruct((row_count, blocks, sub), BF16),
        ),
        grid=(row_count // tile,),
        in_specs=row_specs
        + col_specs
        + [
            pl.BlockSpec((1, times), lambda i: (0, 0)),
            pl.BlockSpec((time_local, times), lambda i: (0, 0)),
        ],
        out_specs=(
            pl.BlockSpec((tile, reps, time_local), lambda i: (i, 0, 0)),
            pl.BlockSpec((tile, blocks, sub), lambda i: (i, 0, 0)),
        ),
        scratch_shapes=[
            pltpu.VMEM((tile * reps, time_local), F32),
            pltpu.VMEM((sub // 128, tile * blocks, 128), F32),
            pltpu.VMEM((reps, tile, times), BF16),
        ],
    )(*[rows] * reps, *[columns] * reps, time_eig[None, :], time_basis)


def per_device(series, space_basis, time_basis, space_eig, time_eig):
    space_count = lax.axis_size("space")
    time_count = lax.axis_size("tm")
    col_block = space_basis.shape[1]
    own = col_block // space_count
    first = lax.axis_index("tm") * col_block + lax.axis_index("space") * own
    space_own = lax.dynamic_slice_in_dim(space_eig, first, own)
    rows, columns = solve_field(
        jnp.transpose(series, (1, 2, 0)),
        space_basis,
        time_basis,
        time_eig[:, None],
        space_own[None, :],
        space_count,
        time_count,
    )
    reps, times = rows.shape[0], rows.shape[-1]
    return grad_and_alpha(
        rows.reshape(reps, -1, times), columns.reshape(reps, space_count, -1, times), time_eig, time_basis
    )


def solution(mesh):
    return jax.shard_map(
        per_device,
        mesh=mesh,
        in_specs=(P("space", None, "tm"), P("space", "tm"), P("tm", None), P(), P()),
        out_specs=(P("space", None, "tm"), P("space", None, "tm")),
        check_vma=False,
    )
```

```python
import functools

import jax
import jax.numpy as jnp
from jax import lax
from jax.experimental import pallas as pl
from jax.experimental.pallas import tpu as pltpu
from jax.sharding import PartitionSpec as P

F32 = jnp.float32
BF16 = jnp.bfloat16
MESH = pl.DeviceIdType.MESH
CONTRACT_LAST = (((1,), (1,)), ((), ()))
CONTRACT_FIRST = (((0,), (0,)), ((), ()))
VMEM_BYTES = 67043328
RING = 4
PIECES = 4
PARTS = 2
LAG = 2


def rcopy(src, dst, send_sem, recv_sem, **where):
    return pltpu.make_async_remote_copy(
        src_ref=src,
        dst_ref=dst,
        send_sem=send_sem,
        recv_sem=recv_sem,
        device_id=where,
        device_id_type=MESH,
    )


def field_kernel(
    space_count,
    time_count,
    series_hbm, basis_hbm, tbasis_hbm, time_eig_ref, space_eig_ref,
    rows_hbm, cols_hbm,
    basis, series, tbasis, pair_out, pair_in, chip_out, chip_in, mine, scaled, partial, below, above, up_out, down_out,
    load_sem, xs_sem, xr_sem, ts_sem, tr_sem, te_sem, ps_sem, pr_sem, cs_sem, cr_sem, gs_sem, gr_sem, fs_sem,
    us_sem, ur_sem, ds_sem, dr_sem, os_sem, ks_sem, kr_sem, kf_sem, ko_sem,
):
    reps, _, time_local, _ = series.shape
    _, blocks, block_rows, times = partial.shape
    own = mine.shape[3]
    pairs = space_count // 2
    last = time_count - 1
    sub_rows = blocks * block_rows // time_count
    me = lax.axis_index("space")
    z = lax.axis_index("tm")
    core = lax.rem(me, 2)
    chip = lax.div(me, 2)
    partner = me + 1 - 2 * core
    total = reps * blocks

    def chip_at(d):
        return lax.bitwise_xor(chip, d)

    def peer(d):
        return 2 * chip_at(d) + core

    barrier = pltpu.get_barrier_semaphore()

    def greet(**where):
        pl.semaphore_signal(barrier, inc=1, device_id=where, device_id_type=MESH)

    @pl.when(z > 0)
    def _():
        greet(tm=z - 1)

    @pl.when(z < last)
    def _():
        greet(tm=z + 1)

    greet(space=partner)
    for d in range(1, pairs):
        greet(space=peer(d))

    loads = [pltpu.make_async_copy(series_hbm.at[q], series.at[q, z], load_sem.at[2 + q]) for q in range(reps)]
    for load in loads:
        load.start()
    share = time_local // pairs
    own_share = pl.ds(pl.multiple_of(chip * share, share), share)
    load_tbasis = pltpu.make_async_copy(tbasis_hbm.at[own_share], tbasis.at[z, own_share], load_sem.at[1])
    load_tbasis.start()
    load_basis = pltpu.make_async_copy(basis_hbm, basis, load_sem.at[0])

    @pl.when(z == 0)
    def _():
        below[...] = jnp.zeros_like(below)

    @pl.when(z == last)
    def _():
        above[...] = jnp.zeros_like(above)

    pl.semaphore_wait(barrier, pairs + jnp.minimum(z, 1) + jnp.minimum(last - z, 1))

    def x_copy(q, j, way, step, p):
        size = series.shape[3] // PARTS
        at = series.at[q, j, :, pl.ds(p * size, size)]
        return rcopy(at, at, xs_sem.at[q, way, step, p], xr_sem.at[q, j, p], tm=z + 1 - 2 * way)

    def t_copy(j, way, step, p):
        at = tbasis.at[j, own_share]
        return rcopy(at, at, ts_sem.at[way, step], tr_sem.at[j], tm=z + 1 - 2 * way)

    def t_share(d):
        at = tbasis.at[:, own_share]
        return rcopy(at, at, te_sem.at[0, d], te_sem.at[1, d], space=peer(d))

    def line_start(line):
        copy, parts = line
        for p in range(parts):
            @pl.when(z < last)
            def _():
                copy(z, 0, 0, p).start()

            @pl.when(z > 0)
            def _():
                copy(z, 1, 0, p).start()

    def line_part(line, k, p):
        copy, _ = line

        @pl.when(z >= k)
        def _():
            copy(z - k, 0, k, p).wait_recv()

            @pl.when(z < last)
            def _():
                copy(z - k, 0, k, p).start()

        @pl.when(z + k <= last)
        def _():
            copy(z + k, 1, k, p).wait_recv()

            @pl.when(z > 0)
            def _():
                copy(z + k, 1, k, p).start()

    def line_step(line, k):
        for p in range(line[1]):
            line_part(line, k, p)

    def line_drain(line):
        copy, parts = line
        for k in range(time_count):
            for p in range(parts):
                @pl.when((z >= k) & (z < last))
                def _():
                    copy(z - k, 0, k, p).wait_send()

                @pl.when((z + k <= last) & (z > 0))
                def _():
                    copy(z + k, 1, k, p).wait_send()

    def x_of(q):
        return functools.partial(x_copy, q), PARTS

    t_line = t_copy, 1

    def pair_copy(q, j, d):
        return rcopy(pair_out.at[d, j], pair_in.at[q, d, j], ps_sem.at[d, j], pr_sem.at[q, d, j], space=partner)

    def chip_copy(q, j, d):
        return rcopy(
            chip_out.at[d - 1, j], chip_in.at[q, d - 1, j], cs_sem.at[d - 1, j], cr_sem.at[q, d - 1, j], space=peer(d)
        )

    def spectrum(q, j, c):
        at = pl.ds(pl.multiple_of(c * own, own), own)
        return jnp.dot(series[q, j], basis[:, at], preferred_element_type=F32)

    def spectral(q, j, send=True):
        @pl.loop(0, pairs)
        def _(n):
            d = pairs - 1 - n
            if q > 0:
                pair_copy(q - 1, j, d).wait_send()
            pair_out[d, j] = spectrum(q, j, 2 * chip_at(d) + 1 - core).astype(BF16)
            pair_copy(q, j, d).start()

        @pl.loop(0, pairs)
        def _(n):
            d = pairs - 1 - n
            value = spectrum(q, j, peer(d))
            pair_copy(q, j, d).wait_recv()
            value = value + pair_in[q, d, j].astype(F32)

            @pl.when(d > 0)
            def _():
                if q > 0:
                    chip_copy(q - 1, j, d).wait_send()
                chip_out[d - 1, j] = value.astype(BF16)
                if send:
                    chip_copy(q, j, d).start()

            @pl.when(d == 0)
            def _():
                mine[q, j] = value

    def spectral_side(q, k, side):
        j = jnp.where(2 * z < time_count, z + k * (1 - 2 * side), z + k * (2 * side - 1))

        @pl.when((j >= 0) & (j <= last))
        def _():
            spectral(q, j)

    def spectral_step(q, k, send=True):
        @pl.loop(0, 2)
        def _(side):
            j = z + k * (2 * side - 1)

            @pl.when((j >= 0) & (j <= last))
            def _():
                spectral(q, j, send)

    def spectral_flush(q, k):
        @pl.loop(0, 2)
        def _(side):
            j = z + k * (2 * side - 1)

            @pl.when((j >= 0) & (j <= last))
            def _():
                for d in reversed(range(1, pairs)):
                    chip_copy(q, j, d).start()

    bits = [1 << b for b in range(pairs.bit_length() - 1)]
    near = [d for d in range(1, pairs) if d in bits]
    turns = [(e, f) for e in bits for f in bits if e != f]
    far = [d for d in range(1, pairs) if d not in bits]
    direct = [d for d in far if d not in [e ^ f for e, f in turns]]

    def piece(q, j, h):
        rows = pl.ds(h * (times // 2), times // 2)
        return scaled.at[q, rows, pl.ds(pl.multiple_of(j * own, own), own)]

    def gather_copy(q, d, h):
        return rcopy(
            piece(q, me, h), piece(q, me, h), gs_sem.at[q, d - 1, h], gr_sem.at[q, me, h], space=peer(d)
        )

    def turn_copy(q, e, f):
        h = 0 if e < f else 1
        at = piece(q, peer(e), h)
        return rcopy(at, at, gs_sem.at[q, (e ^ f) - 1, h], gr_sem.at[q, peer(e), h], space=peer(f))

    def forward_copy(q, j, d, h):
        return rcopy(piece(q, j, h), piece(q, j, h), fs_sem.at[q, d, h], gr_sem.at[q, j, h], space=partner)

    def scale_own(q):
        @pl.loop(0, time_count)
        def _(j):
            for d in range(1, pairs):
                chip_copy(q, j, d).wait_recv()

        value = mine[q]
        for d in range(1, pairs):
            value = value + chip_in[q, d - 1].astype(F32)
        value = value.reshape(time_count * time_local, own)
        rotation = tbasis[...].reshape(time_count * time_local, times)
        turned = lax.dot_general(rotation, value.astype(BF16), CONTRACT_FIRST, preferred_element_type=F32)
        times_eig = jnp.transpose(jnp.broadcast_to(time_eig_ref[...], (8, times)))[:, :1]
        first = pl.multiple_of((z * space_count + me) * own, own)
        turned = turned / (times_eig * space_eig_ref[:, pl.ds(first, own)] + 0.1)
        scaled[q, :, pl.ds(pl.multiple_of(me * own, own), own)] = turned.astype(BF16)
        for h in range(2):
            for d in near + direct:
                gather_copy(q, d, h).start()
            forward_copy(q, me, 0, h).start()

    def gather_near(q):
        for h in range(2):
            for e in near:
                forward_copy(q, peer(e), e, h).wait_recv()
                for f in near:
                    if f != e and h == (0 if e < f else 1):
                        turn_copy(q, e, f).start()
                forward_copy(q, peer(e), e, h).start()

    def gather_far(q):
        for h in range(2):
            for d in far:
                forward_copy(q, peer(d), d, h).wait_recv()
                forward_copy(q, peer(d), d, h).start()

    def gather_finish(q):
        for d in range(pairs):
            for h in range(2):
                forward_copy(q, peer(d) + 1 - 2 * core, d, h).wait_recv()

    def gather_drain(q):
        for h in range(2):
            for d in near + direct:
                gather_copy(q, d, h).wait_send()
            for d in range(pairs):
                forward_copy(q, peer(d), d, h).wait_send()
        for e, f in turns:
            turn_copy(q, e, f).wait_send()

    def back(q, i):
        low = lax.div(i, 2)
        side = lax.rem(i, 2)
        side = jnp.where(2 * z < time_count, side, 1 - side)
        sub = jnp.where(side == 0, last - low, low)
        value = lax.dot_general(
            basis[pl.ds(pl.multiple_of(sub * sub_rows, sub_rows), sub_rows), :],
            scaled[q],
            CONTRACT_LAST,
            preferred_element_type=F32,
        )
        partial[q, pl.ds(sub * PIECES, PIECES)] = value.reshape(PIECES, block_rows, times)

    def up_copy(n, q, m):
        slot = lax.rem(n, RING)
        return rcopy(up_out.at[slot], below.at[q, m], us_sem.at[slot], ur_sem.at[n], tm=z + 1)

    def down_copy(n, q, m):
        slot = lax.rem(n, RING)
        return rcopy(down_out.at[slot], above.at[q, m], ds_sem.at[slot], dr_sem.at[n], tm=z - 1)

    def row_copy(q, m):
        return pltpu.make_async_copy(below.at[q, m], rows_hbm.at[q, m], os_sem.at[q * blocks + m])

    def column_copy(q, p, d):
        source = below.at[q, z * PIECES + p]
        return rcopy(source, cols_hbm.at[q, me, p], ks_sem.at[q, p, d], kr_sem.at[q, me, p], space=peer(d))

    def column_pair(q, p):
        source = below.at[q, z * PIECES + p]
        return rcopy(source, cols_hbm.at[q, me, p], kf_sem.at[q, p, 0], kr_sem.at[q, me, p], space=partner)

    def column_own(q, p):
        return pltpu.make_async_copy(below.at[q, z * PIECES + p], cols_hbm.at[q, me, p], ko_sem.at[q, p])

    def column_forward(q, p, j, d):
        at = cols_hbm.at[q, j, p]
        return rcopy(at, at, kf_sem.at[q, p, d], kr_sem.at[q, j, p], space=partner)

    def columns_start(q, p):
        for d in reversed(range(1, pairs)):
            column_copy(q, p, d).start()
        column_pair(q, p).start()
        column_own(q, p).start()

    def columns_relay(q):
        @pl.loop(0, PIECES)
        def _(n):
            p = jnp.where(2 * z < time_count, PIECES - 1 - n, n)
            p = jnp.where((z == 0) | (z == last), PIECES - 1 - p, p)
            for d in range(1, pairs):
                column_forward(q, p, peer(d), d).wait_recv()
                column_forward(q, p, peer(d), d).start()

    def columns_finish(q):
        @pl.loop(0, PIECES)
        def _(p):
            for d in range(pairs):
                column_forward(q, p, peer(d) + 1 - 2 * core, d).wait_recv()
            for d in range(1, pairs):
                column_copy(q, p, d).wait_send()
                column_forward(q, p, peer(d), d).wait_send()
            column_pair(q, p).wait_send()
            column_own(q, p).wait()

    def finish_block(q, m):
        below[q, m] = (partial[q, m] + below[q, m].astype(F32) + above[q, m].astype(F32)).astype(BF16)
        row_copy(q, m).start()

        @pl.when((lax.div(m, PIECES) == z) & (q == reps - 1))
        def _():
            columns_start(q, lax.rem(m, PIECES))

    def up_step(n):
        at = n - LAG * z

        @pl.when((at >= 0) & (at < total))
        def _():
            q = lax.div(at, blocks)
            m = blocks - 1 - lax.rem(at, blocks)

            @pl.when(z > 0)
            def _():
                up_copy(at, q, m).wait_recv()

            @pl.when(z < last)
            def _():
                @pl.when(at >= RING)
                def _():
                    up_copy(at, q, m).wait_send()

                @pl.when(z == 0)
                def _():
                    up_out[lax.rem(at, RING)] = partial[q, m].astype(BF16)

                @pl.when(z > 0)
                def _():
                    up_out[lax.rem(at, RING)] = (partial[q, m] + below[q, m].astype(F32)).astype(BF16)

                up_copy(at, q, m).start()

            @pl.when((z == last) | ((z > 0) & (q * blocks + m + LAG * (last - z) < n)))
            def _():
                finish_block(q, m)

    def down_step(n):
        at = n - LAG * (last - z)

        @pl.when((at >= 0) & (at < total))
        def _():
            q = lax.div(at, blocks)
            m = lax.rem(at, blocks)

            @pl.when(z < last)
            def _():
                down_copy(at, q, m).wait_recv()

            @pl.when(z > 0)
            def _():
                @pl.when(at >= RING)
                def _():
                    down_copy(at, q, m).wait_send()

                @pl.when(z == last)
                def _():
                    down_out[lax.rem(at, RING)] = partial[q, m].astype(BF16)

                @pl.when(z < last)
                def _():
                    down_out[lax.rem(at, RING)] = (partial[q, m] + above[q, m].astype(F32)).astype(BF16)

                down_copy(at, q, m).start()

            @pl.when((z == 0) | ((z < last) & (q * blocks + blocks - 1 - m + LAG * z <= n)))
            def _():
                finish_block(q, m)

    for load in loads:
        load.wait()
    line_start(x_of(0))
    load_basis.start()
    load_tbasis.wait()
    line_start(t_line)
    load_basis.wait()
    spectral(0, z)
    work = [functools.partial(spectral, q, z) for q in range(1, reps)]
    for k in range(1, time_count):
        for p in range(PARTS):
            if work and k > 1:
                work.pop(0)()
            line_part(x_of(0), k, p)
            if p == PARTS - 1:
                line_step(t_line, k)
                if k == max(1, time_count - 2):
                    for q in range(1, reps):
                        line_start(x_of(q))
            if work and k == 1:
                work.pop(0)()
        while work:
            work.pop(0)()
        work = [functools.partial(spectral_side, 0, k, side) for side in range(2)]
    while work:
        work.pop(0)()
    for d in range(1, pairs):
        t_share(d).start()
    for q in range(reps - 1):
        if q == 0:
            for d in range(1, pairs):
                t_share(d).wait_recv()
        scale_own(q)
        line_step(x_of(q + 1), 1)
        spectral_step(q + 1, 1, False)
        gather_near(q)
        spectral_flush(q + 1, 1)
        for k in range(2, time_count - 1):
            line_step(x_of(q + 1), k)
            spectral_step(q + 1, k)
        gather_far(q)

    ahead = max(7 * blocks // 16, time_count)

    @pl.loop(0, total + LAG * last)
    def _(n):
        q = lax.div(n, blocks)
        i = lax.rem(n, blocks)

        @pl.when((q < reps) & (i < time_count))
        def _():
            @pl.when(i == 0)
            def _():
                gather_finish(q)

            back(q, i)

        up_step(n)
        down_step(n)

        @pl.when((q < reps - 1) & (i == time_count - 1))
        def _():
            for r in range(1, reps):
                @pl.when(q == r - 1)
                def _():
                    for k in range(max(2, time_count - 1), time_count):
                        line_step(x_of(r), k)
                        spectral_step(r, k)

        @pl.when(n == ahead)
        def _():
            scale_own(reps - 1)

        @pl.when(n == (reps - 1) * blocks - 3)
        def _():
            gather_near(reps - 1)

        @pl.when(n == (reps - 1) * blocks - 1)
        def _():
            gather_far(reps - 1)

            @pl.loop(0, PIECES)
            def _(p):
                for r in range(reps - 1):
                    columns_start(r, p)

        @pl.when(n == total - 1)
        def _():
            for r in range(reps - 1):
                columns_relay(r)

    columns_relay(reps - 1)
    for q in range(reps):
        columns_finish(q)
        line_drain(x_of(q))
        gather_drain(q)
    line_drain(t_line)
    for d in range(1, pairs):
        t_share(d).wait_send()
    @pl.loop(0, time_count)
    def _(j):
        for d in range(pairs):
            pair_copy(reps - 1, j, d).wait_send()
            if d > 0:
                chip_copy(reps - 1, j, d).wait_send()

    @pl.loop(0, total)
    def _(n):
        row_copy(lax.div(n, blocks), lax.rem(n, blocks)).wait()

    for n in range(total - min(RING, total), total):
        q, m = n // blocks, n % blocks

        @pl.when(z < last)
        def _():
            up_copy(n, q, m).wait_send()

        @pl.when(z > 0)
        def _():
            down_copy(n, q, m).wait_send()


def solve_field(series, basis, tbasis, time_eig, space_eig, space_count, time_count):
    reps, time_local, rows = series.shape
    depth = basis.shape[1]
    times = tbasis.shape[1]
    own = depth // space_count
    pairs = space_count // 2
    blocks = PIECES * time_count
    block_rows = rows // blocks
    dma = pltpu.SemaphoreType.DMA
    hbm = pl.BlockSpec(memory_space=pl.ANY)
    vmem = pl.BlockSpec(memory_space=pltpu.VMEM)
    return pl.pallas_call(
        functools.partial(field_kernel, space_count, time_count),
        out_shape=(
            jax.ShapeDtypeStruct((reps, blocks, block_rows, times), BF16),
            jax.ShapeDtypeStruct((reps, space_count, PIECES, block_rows, times), BF16),
        ),
        in_specs=[hbm, hbm, hbm, vmem, vmem],
        out_specs=(hbm, hbm),
        scratch_shapes=[
            pltpu.VMEM((rows, depth), BF16),
            pltpu.VMEM((reps, time_count, time_local, rows), BF16),
            pltpu.VMEM((time_count, time_local, times), BF16),
            pltpu.VMEM((pairs, time_count, time_local, own), BF16),
            pltpu.VMEM((reps, pairs, time_count, time_local, own), BF16),
            pltpu.VMEM((pairs - 1, time_count, time_local, own), BF16),
            pltpu.VMEM((reps, pairs - 1, time_count, time_local, own), BF16),
            pltpu.VMEM((reps, time_count, time_local, own), F32),
            pltpu.VMEM((reps, times, depth), BF16),
            pltpu.VMEM((reps, blocks, block_rows, times), F32),
            pltpu.VMEM((reps, blocks, block_rows, times), BF16),
            pltpu.VMEM((reps, blocks, block_rows, times), BF16),
            pltpu.VMEM((RING, block_rows, times), BF16),
            pltpu.VMEM((RING, block_rows, times), BF16),
            dma((2 + reps,)),
            dma((reps, 2, time_count, PARTS)),
            dma((reps, time_count, PARTS)),
            dma((2, time_count)),
            dma((time_count,)),
            dma((2, pairs)),
            dma((pairs, time_count)),
            dma((reps, pairs, time_count)),
            dma((pairs - 1, time_count)),
            dma((reps, pairs - 1, time_count)),
            dma((reps, pairs - 1, 2)),
            dma((reps, space_count, 2)),
            dma((reps, pairs, 2)),
            dma((RING,)),
            dma((reps * blocks,)),
            dma((RING,)),
            dma((reps * blocks,)),
            dma((reps * blocks,)),
            dma((reps, PIECES, pairs)),
            dma((reps, space_count, PIECES)),
            dma((reps, PIECES, pairs)),
            dma((reps, PIECES)),
        ],
        compiler_params=pltpu.CompilerParams(
            collective_id=0, has_side_effects=True, vmem_limit_bytes=VMEM_BYTES
        ),
    )(series, basis, tbasis, time_eig, space_eig)


def grad_kernel(reps, scale, *refs):
    rows, columns = refs[:reps], refs[reps : 2 * reps]
    eig_ref, basis_ref, alpha_ref, grad_ref, alpha_scr, grad_scr, weighted_scr = refs[2 * reps :]
    tile, blocks, _ = grad_ref.shape
    for q in range(reps):
        block = rows[q][0]
        weighted_scr[q] = (block.astype(F32) * eig_ref[...] / scale).astype(BF16)
        alpha_scr[pl.ds(q, tile, stride=reps), :] = lax.dot_general(
            block, basis_ref[...], CONTRACT_LAST, preferred_element_type=F32
        )
    alpha_ref[...] = alpha_scr[...].astype(BF16).reshape(alpha_ref.shape)

    sub = columns[0].shape[2]
    @pl.loop(0, blocks)
    def _(a):
        total = None
        for q in range(reps):
            part = lax.dot_general(
                weighted_scr[q], columns[q][0, a], CONTRACT_LAST, preferred_element_type=F32
            )
            total = part if total is None else total + part
        for w in range(0, sub, 128):
            grad_scr[w // 128, pl.ds(a, tile, stride=blocks), :] = total[:, w : w + 128]
    for w in range(0, sub, 128):
        grad_ref[:, :, w : w + 128] = (
            grad_scr[w // 128].astype(BF16).reshape(tile, blocks, 128)
        )


def grad_and_alpha(rows, columns, time_eig, time_basis):
    reps, row_count, times = rows.shape
    _, blocks, sub, _ = columns.shape
    time_local = time_basis.shape[0]
    tile = min(row_count, 512)
    row_specs = [pl.BlockSpec((1, tile, times), lambda i, q=q: (q, i, 0)) for q in range(reps)]
    col_specs = [pl.BlockSpec((1, blocks, sub, times), lambda i, q=q: (q, 0, 0, 0)) for q in range(reps)]
    return pl.pallas_call(
        lambda *refs: grad_kernel(reps, reps * times, *refs),
        out_shape=(
            jax.ShapeDtypeStruct((row_count, reps, time_local), BF16),
            jax.ShapeDtypeStruct((row_count, blocks, sub), BF16),
        ),
        grid=(row_count // tile,),
        in_specs=row_specs
        + col_specs
        + [
            pl.BlockSpec((1, times), lambda i: (0, 0)),
            pl.BlockSpec((time_local, times), lambda i: (0, 0)),
        ],
        out_specs=(
            pl.BlockSpec((tile, reps, time_local), lambda i: (i, 0, 0)),
            pl.BlockSpec((tile, blocks, sub), lambda i: (i, 0, 0)),
        ),
        scratch_shapes=[
            pltpu.VMEM((tile * reps, time_local), F32),
            pltpu.VMEM((sub // 128, tile * blocks, 128), F32),
            pltpu.VMEM((reps, tile, times), BF16),
        ],
    )(*[rows] * reps, *[columns] * reps, time_eig[None, :], time_basis)


def per_device(series, space_basis, time_basis, space_eig, time_eig):
    space_count = lax.axis_size("space")
    time_count = lax.axis_size("tm")
    rows, columns = solve_field(
        jnp.transpose(series, (1, 2, 0)),
        space_basis,
        time_basis,
        time_eig[None, :],
        space_eig[None, :],
        space_count,
        time_count,
    )
    reps, times = rows.shape[0], rows.shape[-1]
    return grad_and_alpha(
        rows.reshape(reps, -1, times), columns.reshape(reps, space_count, -1, times), time_eig, time_basis
    )


def solution(mesh):
    return jax.shard_map(
        per_device,
        mesh=mesh,
        in_specs=(P("space", None, "tm"), P("space", "tm"), P("tm", None), P(), P()),
        out_specs=(P("space", None, "tm"), P("space", None, "tm")),
        check_vma=False,
    )
```

```python
import functools

import jax
import jax.numpy as jnp
from jax import lax
from jax.experimental import pallas as pl
from jax.experimental.pallas import tpu as pltpu
from jax.sharding import PartitionSpec as P

F32 = jnp.float32
BF16 = jnp.bfloat16
MESH = pl.DeviceIdType.MESH
CONTRACT_LAST = (((1,), (1,)), ((), ()))
CONTRACT_FIRST = (((0,), (0,)), ((), ()))
VMEM_BYTES = 67043328
RING = 4
PIECES = 4
PARTS = 2
LAG = 2


def rcopy(src, dst, send_sem, recv_sem, **where):
    return pltpu.make_async_remote_copy(
        src_ref=src,
        dst_ref=dst,
        send_sem=send_sem,
        recv_sem=recv_sem,
        device_id=where,
        device_id_type=MESH,
    )


def field_kernel(
    space_count,
    time_count,
    series_hbm, basis_hbm, tbasis_hbm, time_eig_ref, space_eig_ref,
    rows_hbm, cols_hbm,
    basis, series, tbasis, pair_out, pair_in, chip_out, chip_in, mine, scaled, partial, below, above, up_out, down_out,
    load_sem, xs_sem, xr_sem, ts_sem, tr_sem, te_sem, ps_sem, pr_sem, cs_sem, cr_sem, gs_sem, gr_sem, fs_sem,
    us_sem, ur_sem, ds_sem, dr_sem, os_sem, ks_sem, kr_sem, kf_sem, ko_sem,
):
    reps, _, time_local, _ = series.shape
    _, blocks, block_rows, times = partial.shape
    own = mine.shape[3]
    pairs = space_count // 2
    last = time_count - 1
    sub_rows = blocks * block_rows // time_count
    me = lax.axis_index("space")
    z = lax.axis_index("tm")
    core = lax.rem(me, 2)
    chip = lax.div(me, 2)
    partner = me + 1 - 2 * core
    total = reps * blocks

    def chip_at(d):
        return lax.bitwise_xor(chip, d)

    def peer(d):
        return 2 * chip_at(d) + core

    barrier = pltpu.get_barrier_semaphore()

    def greet(**where):
        pl.semaphore_signal(barrier, inc=1, device_id=where, device_id_type=MESH)

    @pl.when(z > 0)
    def _():
        greet(tm=z - 1)

    @pl.when(z < last)
    def _():
        greet(tm=z + 1)

    greet(space=partner)
    for d in range(1, pairs):
        greet(space=peer(d))

    loads = [pltpu.make_async_copy(series_hbm.at[q], series.at[q, z], load_sem.at[2 + q]) for q in range(reps)]
    for load in loads:
        load.start()
    share = time_local // pairs
    own_share = pl.ds(pl.multiple_of(chip * share, share), share)
    load_tbasis = pltpu.make_async_copy(tbasis_hbm.at[own_share], tbasis.at[z, own_share], load_sem.at[1])
    load_tbasis.start()
    load_basis = pltpu.make_async_copy(basis_hbm, basis, load_sem.at[0])

    @pl.when(z == 0)
    def _():
        below[...] = jnp.zeros_like(below)

    @pl.when(z == last)
    def _():
        above[...] = jnp.zeros_like(above)

    pl.semaphore_wait(barrier, pairs + jnp.minimum(z, 1) + jnp.minimum(last - z, 1))

    def x_copy(q, j, way, step, p):
        size = series.shape[3] // PARTS
        at = series.at[q, j, :, pl.ds(p * size, size)]
        return rcopy(at, at, xs_sem.at[q, way, step, p], xr_sem.at[q, j, p], tm=z + 1 - 2 * way)

    def t_copy(j, way, step, p):
        at = tbasis.at[j, own_share]
        return rcopy(at, at, ts_sem.at[way, step], tr_sem.at[j], tm=z + 1 - 2 * way)

    def t_share(j, d):
        at = tbasis.at[j, own_share]
        return rcopy(at, at, te_sem.at[0, d, j], te_sem.at[1, d, j], space=peer(d))

    def t_share_step(k):
        @pl.loop(0, 1 if k == 0 else 2)
        def _(side):
            j = z + k * (2 * side - 1)

            @pl.when((j >= 0) & (j <= last))
            def _():
                for d in range(1, pairs):
                    t_share(j, d).start()

    def t_share_each(act):
        @pl.loop(0, time_count)
        def _(j):
            for d in range(1, pairs):
                act(t_share(j, d))

    def line_start(line):
        copy, parts = line
        for p in range(parts):
            @pl.when(z < last)
            def _():
                copy(z, 0, 0, p).start()

            @pl.when(z > 0)
            def _():
                copy(z, 1, 0, p).start()

    def line_part(line, k, p):
        copy, _ = line

        @pl.when(z >= k)
        def _():
            copy(z - k, 0, k, p).wait_recv()

            @pl.when(z < last)
            def _():
                copy(z - k, 0, k, p).start()

        @pl.when(z + k <= last)
        def _():
            copy(z + k, 1, k, p).wait_recv()

            @pl.when(z > 0)
            def _():
                copy(z + k, 1, k, p).start()

    def line_step(line, k):
        for p in range(line[1]):
            line_part(line, k, p)

    def line_drain(line):
        copy, parts = line
        for k in range(time_count):
            for p in range(parts):
                @pl.when((z >= k) & (z < last))
                def _():
                    copy(z - k, 0, k, p).wait_send()

                @pl.when((z + k <= last) & (z > 0))
                def _():
                    copy(z + k, 1, k, p).wait_send()

    def x_of(q):
        return functools.partial(x_copy, q), PARTS

    t_line = t_copy, 1

    def pair_copy(q, j, d):
        return rcopy(pair_out.at[d, j], pair_in.at[q, d, j], ps_sem.at[d, j], pr_sem.at[q, d, j], space=partner)

    def chip_copy(q, j, d):
        return rcopy(
            chip_out.at[d - 1, j], chip_in.at[q, d - 1, j], cs_sem.at[d - 1, j], cr_sem.at[q, d - 1, j], space=peer(d)
        )

    def spectrum(q, j, c):
        at = pl.ds(pl.multiple_of(c * own, own), own)
        return jnp.dot(series[q, j], basis[:, at], preferred_element_type=F32)

    def spectral(q, j, send=True):
        @pl.loop(0, pairs)
        def _(n):
            d = pairs - 1 - n
            if q > 0:
                pair_copy(q - 1, j, d).wait_send()
            pair_out[d, j] = spectrum(q, j, 2 * chip_at(d) + 1 - core).astype(BF16)
            pair_copy(q, j, d).start()

        @pl.loop(0, pairs)
        def _(n):
            d = pairs - 1 - n
            value = spectrum(q, j, peer(d))
            pair_copy(q, j, d).wait_recv()
            value = value + pair_in[q, d, j].astype(F32)

            @pl.when(d > 0)
            def _():
                if q > 0:
                    chip_copy(q - 1, j, d).wait_send()
                chip_out[d - 1, j] = value.astype(BF16)
                if send:
                    chip_copy(q, j, d).start()

            @pl.when(d == 0)
            def _():
                mine[q, j] = value

    def spectral_side(q, k, side):
        j = jnp.where(2 * z < time_count, z + k * (1 - 2 * side), z + k * (2 * side - 1))

        @pl.when((j >= 0) & (j <= last))
        def _():
            spectral(q, j)

    def spectral_step(q, k, send=True):
        @pl.loop(0, 2)
        def _(side):
            j = z + k * (2 * side - 1)

            @pl.when((j >= 0) & (j <= last))
            def _():
                spectral(q, j, send)

    def spectral_flush(q, k):
        @pl.loop(0, 2)
        def _(side):
            j = z + k * (2 * side - 1)

            @pl.when((j >= 0) & (j <= last))
            def _():
                for d in reversed(range(1, pairs)):
                    chip_copy(q, j, d).start()

    bits = [1 << b for b in range(pairs.bit_length() - 1)]
    near = [d for d in range(1, pairs) if d in bits]
    turns = [(e, f) for e in bits for f in bits if e != f]
    far = [d for d in range(1, pairs) if d not in bits]
    direct = [d for d in far if d not in [e ^ f for e, f in turns]]

    def piece(q, j, h):
        rows = pl.ds(h * (times // 2), times // 2)
        return scaled.at[q, rows, pl.ds(pl.multiple_of(j * own, own), own)]

    def gather_copy(q, d, h):
        return rcopy(
            piece(q, me, h), piece(q, me, h), gs_sem.at[q, d - 1, h], gr_sem.at[q, me, h], space=peer(d)
        )

    def turn_copy(q, e, f):
        h = 0 if e < f else 1
        at = piece(q, peer(e), h)
        return rcopy(at, at, gs_sem.at[q, (e ^ f) - 1, h], gr_sem.at[q, peer(e), h], space=peer(f))

    def forward_copy(q, j, d, h):
        return rcopy(piece(q, j, h), piece(q, j, h), fs_sem.at[q, d, h], gr_sem.at[q, j, h], space=partner)

    def scale_own(q):
        @pl.loop(0, time_count)
        def _(j):
            for d in range(1, pairs):
                chip_copy(q, j, d).wait_recv()

        value = mine[q]
        for d in range(1, pairs):
            value = value + chip_in[q, d - 1].astype(F32)
        value = value.reshape(time_count * time_local, own)
        rotation = tbasis[...].reshape(time_count * time_local, times)
        turned = lax.dot_general(rotation, value.astype(BF16), CONTRACT_FIRST, preferred_element_type=F32)
        times_eig = jnp.transpose(jnp.broadcast_to(time_eig_ref[...], (8, times)))[:, :1]
        first = pl.multiple_of((z * space_count + me) * own, own)
        turned = turned / (times_eig * space_eig_ref[:, pl.ds(first, own)] + 0.1)
        scaled[q, :, pl.ds(pl.multiple_of(me * own, own), own)] = turned.astype(BF16)
        for h in range(2):
            for d in near + direct:
                gather_copy(q, d, h).start()
            forward_copy(q, me, 0, h).start()

    def gather_near(q):
        for h in range(2):
            for e in near:
                forward_copy(q, peer(e), e, h).wait_recv()
                for f in near:
                    if f != e and h == (0 if e < f else 1):
                        turn_copy(q, e, f).start()
                forward_copy(q, peer(e), e, h).start()

    def gather_far(q):
        for h in range(2):
            for d in far:
                forward_copy(q, peer(d), d, h).wait_recv()
                forward_copy(q, peer(d), d, h).start()

    def gather_finish(q):
        for d in range(pairs):
            for h in range(2):
                forward_copy(q, peer(d) + 1 - 2 * core, d, h).wait_recv()

    def gather_drain(q):
        for h in range(2):
            for d in near + direct:
                gather_copy(q, d, h).wait_send()
            for d in range(pairs):
                forward_copy(q, peer(d), d, h).wait_send()
        for e, f in turns:
            turn_copy(q, e, f).wait_send()

    def back(q, i):
        low = lax.div(i, 2)
        side = lax.rem(i, 2)
        side = jnp.where(2 * z < time_count, side, 1 - side)
        sub = jnp.where(side == 0, last - low, low)
        value = lax.dot_general(
            basis[pl.ds(pl.multiple_of(sub * sub_rows, sub_rows), sub_rows), :],
            scaled[q],
            CONTRACT_LAST,
            preferred_element_type=F32,
        )
        partial[q, pl.ds(sub * PIECES, PIECES)] = value.reshape(PIECES, block_rows, times)

    def up_copy(n, q, m):
        slot = lax.rem(n, RING)
        return rcopy(up_out.at[slot], below.at[q, m], us_sem.at[slot], ur_sem.at[n], tm=z + 1)

    def down_copy(n, q, m):
        slot = lax.rem(n, RING)
        return rcopy(down_out.at[slot], above.at[q, m], ds_sem.at[slot], dr_sem.at[n], tm=z - 1)

    def rep_columns(q):
        return pl.ds(pl.multiple_of(q * times, times), times)

    def row_copy(q, m):
        return pltpu.make_async_copy(below.at[q, m], rows_hbm.at[m, :, rep_columns(q)], os_sem.at[q * blocks + m])

    def column_at(q, p, j):
        return cols_hbm.at[j, p, :, rep_columns(q)]

    def column_copy(q, p, d):
        source = below.at[q, z * PIECES + p]
        return rcopy(source, column_at(q, p, me), ks_sem.at[q, p, d], kr_sem.at[q, me, p], space=peer(d))

    def column_pair(q, p):
        source = below.at[q, z * PIECES + p]
        return rcopy(source, column_at(q, p, me), kf_sem.at[q, p, 0], kr_sem.at[q, me, p], space=partner)

    def column_own(q, p):
        return pltpu.make_async_copy(below.at[q, z * PIECES + p], column_at(q, p, me), ko_sem.at[q, p])

    def column_forward(q, p, j, d):
        at = column_at(q, p, j)
        return rcopy(at, at, kf_sem.at[q, p, d], kr_sem.at[q, j, p], space=partner)

    def columns_start(q, p):
        for d in reversed(range(1, pairs)):
            column_copy(q, p, d).start()
        column_pair(q, p).start()
        column_own(q, p).start()

    def columns_relay(q):
        @pl.loop(0, PIECES)
        def _(n):
            p = jnp.where(2 * z < time_count, PIECES - 1 - n, n)
            p = jnp.where((z == 0) | (z == last), PIECES - 1 - p, p)
            for d in range(1, pairs):
                column_forward(q, p, peer(d), d).wait_recv()
                column_forward(q, p, peer(d), d).start()

    def columns_finish(q):
        @pl.loop(0, PIECES)
        def _(p):
            for d in range(pairs):
                column_forward(q, p, peer(d) + 1 - 2 * core, d).wait_recv()
            for d in range(1, pairs):
                column_copy(q, p, d).wait_send()
                column_forward(q, p, peer(d), d).wait_send()
            column_pair(q, p).wait_send()
            column_own(q, p).wait()

    def finish_block(q, m):
        below[q, m] = (partial[q, m] + below[q, m].astype(F32) + above[q, m].astype(F32)).astype(BF16)
        row_copy(q, m).start()

        @pl.when((lax.div(m, PIECES) == z) & (q == reps - 1))
        def _():
            columns_start(q, lax.rem(m, PIECES))

    def up_step(n):
        at = n - LAG * z

        @pl.when((at >= 0) & (at < total))
        def _():
            q = lax.div(at, blocks)
            m = blocks - 1 - lax.rem(at, blocks)

            @pl.when(z > 0)
            def _():
                up_copy(at, q, m).wait_recv()

            @pl.when(z < last)
            def _():
                @pl.when(at >= RING)
                def _():
                    up_copy(at, q, m).wait_send()

                @pl.when(z == 0)
                def _():
                    up_out[lax.rem(at, RING)] = partial[q, m].astype(BF16)

                @pl.when(z > 0)
                def _():
                    up_out[lax.rem(at, RING)] = (partial[q, m] + below[q, m].astype(F32)).astype(BF16)

                up_copy(at, q, m).start()

            @pl.when((z == last) | ((z > 0) & (q * blocks + m + LAG * (last - z) < n)))
            def _():
                finish_block(q, m)

    def down_step(n):
        at = n - LAG * (last - z)

        @pl.when((at >= 0) & (at < total))
        def _():
            q = lax.div(at, blocks)
            m = lax.rem(at, blocks)

            @pl.when(z < last)
            def _():
                down_copy(at, q, m).wait_recv()

            @pl.when(z > 0)
            def _():
                @pl.when(at >= RING)
                def _():
                    down_copy(at, q, m).wait_send()

                @pl.when(z == last)
                def _():
                    down_out[lax.rem(at, RING)] = partial[q, m].astype(BF16)

                @pl.when(z < last)
                def _():
                    down_out[lax.rem(at, RING)] = (partial[q, m] + above[q, m].astype(F32)).astype(BF16)

                down_copy(at, q, m).start()

            @pl.when((z == 0) | ((z < last) & (q * blocks + blocks - 1 - m + LAG * z <= n)))
            def _():
                finish_block(q, m)

    for load in loads:
        load.wait()
    line_start(x_of(0))
    load_basis.start()
    load_tbasis.wait()
    line_start(t_line)
    t_share_step(0)
    load_basis.wait()
    spectral(0, z)
    work = [functools.partial(spectral, q, z) for q in range(1, reps)]
    for k in range(1, time_count):
        for p in range(PARTS):
            if work and k > 1:
                work.pop(0)()
            line_part(x_of(0), k, p)
            if p == PARTS - 1:
                line_step(t_line, k)
                t_share_step(k)
                if k == max(1, time_count - 2):
                    for q in range(1, reps):
                        line_start(x_of(q))
            if work and k == 1:
                work.pop(0)()
        while work:
            work.pop(0)()
        work = [functools.partial(spectral_side, 0, k, side) for side in range(2)]
    while work:
        work.pop(0)()
    for q in range(reps - 1):
        if q == 0:
            t_share_each(lambda copy: copy.wait_recv())
        scale_own(q)
        line_step(x_of(q + 1), 1)
        spectral_step(q + 1, 1, False)
        gather_near(q)
        spectral_flush(q + 1, 1)
        for k in range(2, time_count - 1):
            line_step(x_of(q + 1), k)
            spectral_step(q + 1, k)
        gather_far(q)

    ahead = max(7 * blocks // 16, time_count)

    @pl.loop(0, total + LAG * last)
    def _(n):
        q = lax.div(n, blocks)
        i = lax.rem(n, blocks)

        @pl.when((q < reps) & (i < time_count))
        def _():
            @pl.when(i == 0)
            def _():
                gather_finish(q)

            back(q, i)

        up_step(n)
        down_step(n)

        @pl.when((q < reps - 1) & (i == time_count - 1))
        def _():
            for r in range(1, reps):
                @pl.when(q == r - 1)
                def _():
                    for k in range(max(2, time_count - 1), time_count):
                        line_step(x_of(r), k)
                        spectral_step(r, k)

        @pl.when(n == ahead)
        def _():
            scale_own(reps - 1)

        @pl.when(n == (reps - 1) * blocks - 3)
        def _():
            gather_near(reps - 1)

        @pl.when(n == (reps - 1) * blocks - 1)
        def _():
            gather_far(reps - 1)

            @pl.loop(0, PIECES)
            def _(p):
                for r in range(reps - 1):
                    columns_start(r, p)

        @pl.when(n == total - 1)
        def _():
            for r in range(reps - 1):
                columns_relay(r)

    columns_relay(reps - 1)
    for q in range(reps):
        columns_finish(q)
        line_drain(x_of(q))
        gather_drain(q)
    line_drain(t_line)
    t_share_each(lambda copy: copy.wait_send())
    @pl.loop(0, time_count)
    def _(j):
        for d in range(pairs):
            pair_copy(reps - 1, j, d).wait_send()
            if d > 0:
                chip_copy(reps - 1, j, d).wait_send()

    @pl.loop(0, total)
    def _(n):
        row_copy(lax.div(n, blocks), lax.rem(n, blocks)).wait()

    for n in range(total - min(RING, total), total):
        q, m = n // blocks, n % blocks

        @pl.when(z < last)
        def _():
            up_copy(n, q, m).wait_send()

        @pl.when(z > 0)
        def _():
            down_copy(n, q, m).wait_send()


def solve_field(series, basis, tbasis, time_eig, space_eig, space_count, time_count):
    reps, time_local, rows = series.shape
    depth = basis.shape[1]
    times = tbasis.shape[1]
    own = depth // space_count
    pairs = space_count // 2
    blocks = PIECES * time_count
    block_rows = rows // blocks
    dma = pltpu.SemaphoreType.DMA
    hbm = pl.BlockSpec(memory_space=pl.ANY)
    vmem = pl.BlockSpec(memory_space=pltpu.VMEM)
    return pl.pallas_call(
        functools.partial(field_kernel, space_count, time_count),
        out_shape=(
            jax.ShapeDtypeStruct((blocks, block_rows, reps * times), BF16),
            jax.ShapeDtypeStruct((space_count, PIECES, block_rows, reps * times), BF16),
        ),
        in_specs=[hbm, hbm, hbm, vmem, vmem],
        out_specs=(hbm, hbm),
        scratch_shapes=[
            pltpu.VMEM((rows, depth), BF16),
            pltpu.VMEM((reps, time_count, time_local, rows), BF16),
            pltpu.VMEM((time_count, time_local, times), BF16),
            pltpu.VMEM((pairs, time_count, time_local, own), BF16),
            pltpu.VMEM((reps, pairs, time_count, time_local, own), BF16),
            pltpu.VMEM((pairs - 1, time_count, time_local, own), BF16),
            pltpu.VMEM((reps, pairs - 1, time_count, time_local, own), BF16),
            pltpu.VMEM((reps, time_count, time_local, own), F32),
            pltpu.VMEM((reps, times, depth), BF16),
            pltpu.VMEM((reps, blocks, block_rows, times), F32),
            pltpu.VMEM((reps, blocks, block_rows, times), BF16),
            pltpu.VMEM((reps, blocks, block_rows, times), BF16),
            pltpu.VMEM((RING, block_rows, times), BF16),
            pltpu.VMEM((RING, block_rows, times), BF16),
            dma((2 + reps,)),
            dma((reps, 2, time_count, PARTS)),
            dma((reps, time_count, PARTS)),
            dma((2, time_count)),
            dma((time_count,)),
            dma((2, pairs, time_count)),
            dma((pairs, time_count)),
            dma((reps, pairs, time_count)),
            dma((pairs - 1, time_count)),
            dma((reps, pairs - 1, time_count)),
            dma((reps, pairs - 1, 2)),
            dma((reps, space_count, 2)),
            dma((reps, pairs, 2)),
            dma((RING,)),
            dma((reps * blocks,)),
            dma((RING,)),
            dma((reps * blocks,)),
            dma((reps * blocks,)),
            dma((reps, PIECES, pairs)),
            dma((reps, space_count, PIECES)),
            dma((reps, PIECES, pairs)),
            dma((reps, PIECES)),
        ],
        compiler_params=pltpu.CompilerParams(
            collective_id=0, has_side_effects=True, vmem_limit_bytes=VMEM_BYTES
        ),
    )(series, basis, tbasis, time_eig, space_eig)


def grad_kernel(reps, wide, rows, columns, eig_ref, basis_ref, alpha_ref, grad_ref, alpha_scr, weighted, *halves):
    tile, blocks, sub = grad_ref.shape
    depth = rows.shape[1]
    times = depth // reps
    weighted[...] = (rows[...].astype(F32) * eig_ref[...] / depth).astype(BF16)
    for q in range(reps):
        alpha_scr[pl.ds(q, tile, stride=reps), :] = lax.dot_general(
            rows[:, q * times : (q + 1) * times], basis_ref[...], CONTRACT_LAST, preferred_element_type=F32
        )
    alpha_ref[...] = alpha_scr[...].astype(BF16).reshape(alpha_ref.shape)
    for w in range(0, sub, wide):
        half = halves[w // wide % 2]
        for a in range(blocks):
            part = lax.dot_general(
                weighted[...], columns[a, w : w + wide, :], CONTRACT_LAST, preferred_element_type=F32
            )
            for v in range(0, wide, 128):
                half[v // 128, pl.ds(a, tile, stride=blocks), :] = part[:, v : v + 128]
        for v in range(0, wide, 128):
            grad_ref[:, :, w + v : w + v + 128] = half[v // 128].astype(BF16).reshape(tile, blocks, 128)


def grad_and_alpha(rows, columns, time_eig, time_basis, reps):
    row_count, depth = rows.shape
    blocks, sub, _ = columns.shape
    time_local, times = time_basis.shape
    tile = min(row_count, 256)
    wide = min(sub, 256)
    return pl.pallas_call(
        functools.partial(grad_kernel, reps, wide),
        out_shape=(
            jax.ShapeDtypeStruct((row_count, reps, time_local), BF16),
            jax.ShapeDtypeStruct((row_count, blocks, sub), BF16),
        ),
        grid=(row_count // tile,),
        in_specs=[
            pl.BlockSpec((tile, depth), lambda i: (i, 0)),
            pl.BlockSpec((blocks, sub, depth), lambda i: (0, 0, 0)),
            pl.BlockSpec((1, depth), lambda i: (0, 0)),
            pl.BlockSpec((time_local, times), lambda i: (0, 0)),
        ],
        out_specs=(
            pl.BlockSpec((tile, reps, time_local), lambda i: (i, 0, 0)),
            pl.BlockSpec((tile, blocks, sub), lambda i: (i, 0, 0)),
        ),
        scratch_shapes=[
            pltpu.VMEM((tile * reps, time_local), F32),
            pltpu.VMEM((tile, depth), BF16),
            pltpu.VMEM((wide // 128, tile * blocks, 128), F32),
            pltpu.VMEM((wide // 128, tile * blocks, 128), F32),
        ],
    )(rows, columns, jnp.tile(time_eig, reps)[None, :], time_basis)


def per_device(series, space_basis, time_basis, space_eig, time_eig):
    space_count = lax.axis_size("space")
    time_count = lax.axis_size("tm")
    rows, columns = solve_field(
        jnp.transpose(series, (1, 2, 0)),
        space_basis,
        time_basis,
        time_eig[None, :],
        space_eig[None, :],
        space_count,
        time_count,
    )
    depth = rows.shape[-1]
    return grad_and_alpha(
        rows.reshape(-1, depth), columns.reshape(space_count, -1, depth), time_eig, time_basis, series.shape[1]
    )


def solution(mesh):
    return jax.shard_map(
        per_device,
        mesh=mesh,
        in_specs=(P("space", None, "tm"), P("space", "tm"), P("tm", None), P(), P()),
        out_specs=(P("space", None, "tm"), P("space", None, "tm")),
        check_vma=False,
    )
```

```python
import functools

import jax
import jax.numpy as jnp
from jax import lax
from jax.experimental import pallas as pl
from jax.experimental.pallas import tpu as pltpu
from jax.sharding import PartitionSpec as P

F32 = jnp.float32
BF16 = jnp.bfloat16
MESH = pl.DeviceIdType.MESH
CONTRACT_LAST = (((1,), (1,)), ((), ()))
CONTRACT_FIRST = (((0,), (0,)), ((), ()))
VMEM_BYTES = 67043328
RING = 4
PIECES = 2
PARTS = 2
HALVES = 2
LAG = 2


def rcopy(src, dst, send_sem, recv_sem, **where):
    return pltpu.make_async_remote_copy(
        src_ref=src,
        dst_ref=dst,
        send_sem=send_sem,
        recv_sem=recv_sem,
        device_id=where,
        device_id_type=MESH,
    )


def field_kernel(
    space_count,
    time_count,
    series_hbm, basis_hbm, tbasis_hbm, time_eig_ref, space_eig_ref,
    rows_hbm, cols_hbm,
    basis, series, tbasis, pair_out, pair_in, chip_out, chip_in, mine, scaled, partial, below, above, up_out, down_out,
    load_sem, xs_sem, xr_sem, ts_sem, tr_sem, te_sem, ps_sem, pr_sem, cs_sem, cr_sem, gs_sem, gr_sem, fs_sem,
    us_sem, ur_sem, ds_sem, dr_sem, os_sem, ks_sem, kr_sem, kf_sem, ko_sem,
):
    reps, _, time_local, _ = series.shape
    streams, blocks, block_rows, width = partial.shape
    times = width * HALVES
    own = mine.shape[3]
    pairs = space_count // 2
    last = time_count - 1
    sub_rows = blocks * block_rows // time_count
    me = lax.axis_index("space")
    z = lax.axis_index("tm")
    core = lax.rem(me, 2)
    chip = lax.div(me, 2)
    partner = me + 1 - 2 * core
    total = streams * blocks

    def chip_at(d):
        return lax.bitwise_xor(chip, d)

    def peer(d):
        return 2 * chip_at(d) + core

    barrier = pltpu.get_barrier_semaphore()

    def greet(**where):
        pl.semaphore_signal(barrier, inc=1, device_id=where, device_id_type=MESH)

    @pl.when(z > 0)
    def _():
        greet(tm=z - 1)

    @pl.when(z < last)
    def _():
        greet(tm=z + 1)

    greet(space=partner)
    for d in range(1, pairs):
        greet(space=peer(d))

    loads = [pltpu.make_async_copy(series_hbm.at[q], series.at[q, z], load_sem.at[2 + q]) for q in range(reps)]
    for load in loads:
        load.start()
    share = time_local // pairs
    own_share = pl.ds(pl.multiple_of(chip * share, share), share)
    load_tbasis = pltpu.make_async_copy(tbasis_hbm.at[own_share], tbasis.at[z, own_share], load_sem.at[1])
    load_tbasis.start()
    load_basis = pltpu.make_async_copy(basis_hbm, basis, load_sem.at[0])

    @pl.when(z == 0)
    def _():
        below[...] = jnp.zeros_like(below)

    @pl.when(z == last)
    def _():
        above[...] = jnp.zeros_like(above)

    pl.semaphore_wait(barrier, pairs + jnp.minimum(z, 1) + jnp.minimum(last - z, 1))

    def x_copy(q, j, way, step, p):
        size = series.shape[3] // PARTS
        at = series.at[q, j, :, pl.ds(p * size, size)]
        return rcopy(at, at, xs_sem.at[q, way, step, p], xr_sem.at[q, j, p], tm=z + 1 - 2 * way)

    def t_copy(j, way, step, p):
        at = tbasis.at[j, own_share]
        return rcopy(at, at, ts_sem.at[way, step], tr_sem.at[j], tm=z + 1 - 2 * way)

    def t_share(j, d):
        at = tbasis.at[j, own_share]
        return rcopy(at, at, te_sem.at[0, d, j], te_sem.at[1, d, j], space=peer(d))

    def t_share_step(k):
        @pl.loop(0, 1 if k == 0 else 2)
        def _(side):
            j = z + k * (2 * side - 1)

            @pl.when((j >= 0) & (j <= last))
            def _():
                for d in range(1, pairs):
                    t_share(j, d).start()

    def t_share_each(act):
        @pl.loop(0, time_count)
        def _(j):
            for d in range(1, pairs):
                act(t_share(j, d))

    def line_start(line):
        copy, parts = line
        for p in range(parts):
            @pl.when(z < last)
            def _():
                copy(z, 0, 0, p).start()

            @pl.when(z > 0)
            def _():
                copy(z, 1, 0, p).start()

    def line_part(line, k, p):
        copy, _ = line

        @pl.when(z >= k)
        def _():
            copy(z - k, 0, k, p).wait_recv()

            @pl.when(z < last)
            def _():
                copy(z - k, 0, k, p).start()

        @pl.when(z + k <= last)
        def _():
            copy(z + k, 1, k, p).wait_recv()

            @pl.when(z > 0)
            def _():
                copy(z + k, 1, k, p).start()

    def line_step(line, k):
        for p in range(line[1]):
            line_part(line, k, p)

    def line_drain(line):
        copy, parts = line
        for k in range(time_count):
            for p in range(parts):
                @pl.when((z >= k) & (z < last))
                def _():
                    copy(z - k, 0, k, p).wait_send()

                @pl.when((z + k <= last) & (z > 0))
                def _():
                    copy(z + k, 1, k, p).wait_send()

    def x_of(q):
        return functools.partial(x_copy, q), PARTS

    t_line = t_copy, 1

    def pair_copy(q, j, d):
        return rcopy(pair_out.at[d, j], pair_in.at[q, d, j], ps_sem.at[d, j], pr_sem.at[q, d, j], space=partner)

    def chip_copy(q, j, d):
        return rcopy(
            chip_out.at[d - 1, j], chip_in.at[q, d - 1, j], cs_sem.at[d - 1, j], cr_sem.at[q, d - 1, j], space=peer(d)
        )

    def spectrum(q, j, c):
        at = pl.ds(pl.multiple_of(c * own, own), own)
        return jnp.dot(series[q, j], basis[:, at], preferred_element_type=F32)

    def spectral(q, j, send=True):
        @pl.loop(0, pairs)
        def _(n):
            d = pairs - 1 - n
            if q > 0:
                pair_copy(q - 1, j, d).wait_send()
            pair_out[d, j] = spectrum(q, j, 2 * chip_at(d) + 1 - core).astype(BF16)
            pair_copy(q, j, d).start()

        @pl.loop(0, pairs)
        def _(n):
            d = pairs - 1 - n
            value = spectrum(q, j, peer(d))
            pair_copy(q, j, d).wait_recv()
            value = value + pair_in[q, d, j].astype(F32)

            @pl.when(d > 0)
            def _():
                if q > 0:
                    chip_copy(q - 1, j, d).wait_send()
                chip_out[d - 1, j] = value.astype(BF16)
                if send:
                    chip_copy(q, j, d).start()

            @pl.when(d == 0)
            def _():
                mine[q, j] = value

    def spectral_side(q, k, side):
        j = jnp.where(2 * z < time_count, z + k * (1 - 2 * side), z + k * (2 * side - 1))

        @pl.when((j >= 0) & (j <= last))
        def _():
            spectral(q, j)

    def spectral_step(q, k, send=True):
        @pl.loop(0, 2)
        def _(side):
            j = z + k * (2 * side - 1)

            @pl.when((j >= 0) & (j <= last))
            def _():
                spectral(q, j, send)

    def spectral_flush(q, k):
        @pl.loop(0, 2)
        def _(side):
            j = z + k * (2 * side - 1)

            @pl.when((j >= 0) & (j <= last))
            def _():
                for d in reversed(range(1, pairs)):
                    chip_copy(q, j, d).start()

    bits = [1 << b for b in range(pairs.bit_length() - 1)]
    near = [d for d in range(1, pairs) if d in bits]
    turns = [(e, f) for e in bits for f in bits if e != f]
    far = [d for d in range(1, pairs) if d not in bits]
    direct = [d for d in far if d not in [e ^ f for e, f in turns]]

    def piece(v, j, g):
        rows = pl.ds(g * (width // 2), width // 2)
        return scaled.at[v, rows, pl.ds(pl.multiple_of(j * own, own), own)]

    def gather_copy(v, d, g):
        return rcopy(
            piece(v, me, g), piece(v, me, g), gs_sem.at[v, d - 1, g], gr_sem.at[v, me, g], space=peer(d)
        )

    def turn_copy(v, e, f):
        g = 0 if e < f else 1
        at = piece(v, peer(e), g)
        return rcopy(at, at, gs_sem.at[v, (e ^ f) - 1, g], gr_sem.at[v, peer(e), g], space=peer(f))

    def forward_copy(v, j, d, g):
        return rcopy(piece(v, j, g), piece(v, j, g), fs_sem.at[v, d, g], gr_sem.at[v, j, g], space=partner)

    def scale_own(q):
        @pl.loop(0, time_count)
        def _(j):
            for d in range(1, pairs):
                chip_copy(q, j, d).wait_recv()

        value = mine[q]
        for d in range(1, pairs):
            value = value + chip_in[q, d - 1].astype(F32)
        value = value.reshape(time_count * time_local, own)
        rotation = tbasis[...].reshape(time_count * time_local, times)
        turned = lax.dot_general(rotation, value.astype(BF16), CONTRACT_FIRST, preferred_element_type=F32)
        times_eig = jnp.transpose(jnp.broadcast_to(time_eig_ref[...], (8, times)))[:, :1]
        first = pl.multiple_of((z * space_count + me) * own, own)
        turned = turned / (times_eig * space_eig_ref[:, pl.ds(first, own)] + 0.1)
        for h in range(HALVES):
            scaled[q * HALVES + h, :, pl.ds(pl.multiple_of(me * own, own), own)] = turned[
                h * width : (h + 1) * width
            ].astype(BF16)

    def gather_start(v):
        for g in range(2):
            for d in near + direct:
                gather_copy(v, d, g).start()
            forward_copy(v, me, 0, g).start()

    def gather_near(v):
        for g in range(2):
            for e in near:
                forward_copy(v, peer(e), e, g).wait_recv()
                for f in near:
                    if f != e and g == (0 if e < f else 1):
                        turn_copy(v, e, f).start()
                forward_copy(v, peer(e), e, g).start()

    def gather_far(v):
        for g in range(2):
            for d in far:
                forward_copy(v, peer(d), d, g).wait_recv()
                forward_copy(v, peer(d), d, g).start()

    def gather_finish(v):
        for d in range(pairs):
            for g in range(2):
                forward_copy(v, peer(d) + 1 - 2 * core, d, g).wait_recv()

    def gather_drain(v):
        for g in range(2):
            for d in near + direct:
                gather_copy(v, d, g).wait_send()
            for d in range(pairs):
                forward_copy(v, peer(d), d, g).wait_send()
        for e, f in turns:
            turn_copy(v, e, f).wait_send()

    def back(q, i):
        low = lax.div(i, 2)
        side = lax.rem(i, 2)
        side = jnp.where(2 * z < time_count, side, 1 - side)
        sub = jnp.where(side == 0, last - low, low)
        value = lax.dot_general(
            basis[pl.ds(pl.multiple_of(sub * sub_rows, sub_rows), sub_rows), :],
            scaled[q],
            CONTRACT_LAST,
            preferred_element_type=F32,
        )
        partial[q, pl.ds(sub * PIECES, PIECES)] = value.reshape(PIECES, block_rows, width)

    def up_copy(n, q, m):
        slot = lax.rem(n, RING)
        return rcopy(up_out.at[slot], below.at[q, m], us_sem.at[slot], ur_sem.at[n], tm=z + 1)

    def down_copy(n, q, m):
        slot = lax.rem(n, RING)
        return rcopy(down_out.at[slot], above.at[q, m], ds_sem.at[slot], dr_sem.at[n], tm=z - 1)

    def rep_columns(q):
        return pl.ds(pl.multiple_of(q * width, width), width)

    def row_copy(q, m):
        return pltpu.make_async_copy(below.at[q, m], rows_hbm.at[m, :, rep_columns(q)], os_sem.at[q * blocks + m])

    def column_at(q, p, j):
        return cols_hbm.at[j, p, :, rep_columns(q)]

    def column_copy(q, p, d):
        source = below.at[q, z * PIECES + p]
        return rcopy(source, column_at(q, p, me), ks_sem.at[q, p, d], kr_sem.at[q, me, p], space=peer(d))

    def column_pair(q, p):
        source = below.at[q, z * PIECES + p]
        return rcopy(source, column_at(q, p, me), kf_sem.at[q, p, 0], kr_sem.at[q, me, p], space=partner)

    def column_own(q, p):
        return pltpu.make_async_copy(below.at[q, z * PIECES + p], column_at(q, p, me), ko_sem.at[q, p])

    def column_forward(q, p, j, d):
        at = column_at(q, p, j)
        return rcopy(at, at, kf_sem.at[q, p, d], kr_sem.at[q, j, p], space=partner)

    def columns_start(q, p):
        for d in reversed(range(1, pairs)):
            column_copy(q, p, d).start()
        column_pair(q, p).start()
        column_own(q, p).start()

    def columns_relay(q):
        @pl.loop(0, PIECES)
        def _(n):
            p = jnp.where(2 * z < time_count, PIECES - 1 - n, n)
            p = jnp.where((z == 0) | (z == last), PIECES - 1 - p, p)
            for d in range(1, pairs):
                column_forward(q, p, peer(d), d).wait_recv()
                column_forward(q, p, peer(d), d).start()

    def columns_finish(q):
        @pl.loop(0, PIECES)
        def _(p):
            for d in range(pairs):
                column_forward(q, p, peer(d) + 1 - 2 * core, d).wait_recv()
            for d in range(1, pairs):
                column_copy(q, p, d).wait_send()
                column_forward(q, p, peer(d), d).wait_send()
            column_pair(q, p).wait_send()
            column_own(q, p).wait()

    def finish_block(q, m):
        below[q, m] = (partial[q, m] + below[q, m].astype(F32) + above[q, m].astype(F32)).astype(BF16)
        row_copy(q, m).start()

        @pl.when((lax.div(m, PIECES) == z) & (q == streams - 1))
        def _():
            columns_start(q, lax.rem(m, PIECES))

    def up_step(n):
        at = n - LAG * z

        @pl.when((at >= 0) & (at < total))
        def _():
            q = lax.div(at, blocks)
            m = blocks - 1 - lax.rem(at, blocks)

            @pl.when(z > 0)
            def _():
                up_copy(at, q, m).wait_recv()

            @pl.when(z < last)
            def _():
                @pl.when(at >= RING)
                def _():
                    up_copy(at, q, m).wait_send()

                @pl.when(z == 0)
                def _():
                    up_out[lax.rem(at, RING)] = partial[q, m].astype(BF16)

                @pl.when(z > 0)
                def _():
                    up_out[lax.rem(at, RING)] = (partial[q, m] + below[q, m].astype(F32)).astype(BF16)

                up_copy(at, q, m).start()

            @pl.when((z == last) | ((z > 0) & (q * blocks + m + LAG * (last - z) < n)))
            def _():
                finish_block(q, m)

    def down_step(n):
        at = n - LAG * (last - z)

        @pl.when((at >= 0) & (at < total))
        def _():
            q = lax.div(at, blocks)
            m = lax.rem(at, blocks)

            @pl.when(z < last)
            def _():
                down_copy(at, q, m).wait_recv()

            @pl.when(z > 0)
            def _():
                @pl.when(at >= RING)
                def _():
                    down_copy(at, q, m).wait_send()

                @pl.when(z == last)
                def _():
                    down_out[lax.rem(at, RING)] = partial[q, m].astype(BF16)

                @pl.when(z < last)
                def _():
                    down_out[lax.rem(at, RING)] = (partial[q, m] + above[q, m].astype(F32)).astype(BF16)

                down_copy(at, q, m).start()

            @pl.when((z == 0) | ((z < last) & (q * blocks + blocks - 1 - m + LAG * z <= n)))
            def _():
                finish_block(q, m)

    for load in loads:
        load.wait()
    line_start(x_of(0))
    load_basis.start()
    load_tbasis.wait()
    line_start(t_line)
    t_share_step(0)
    load_basis.wait()
    spectral(0, z)
    work = [functools.partial(spectral, q, z) for q in range(1, reps)]
    for k in range(1, time_count):
        for p in range(PARTS):
            if work and k > 1:
                work.pop(0)()
            line_part(x_of(0), k, p)
            if p == PARTS - 1:
                line_step(t_line, k)
                t_share_step(k)
                if k == max(1, time_count - 2):
                    for q in range(1, reps):
                        line_start(x_of(q))
            if work and k == 1:
                work.pop(0)()
        while work:
            work.pop(0)()
        work = [functools.partial(spectral_side, 0, k, side) for side in range(2)]
    while work:
        work.pop(0)()
    for q in range(reps - 1):
        if q == 0:
            t_share_each(lambda copy: copy.wait_recv())
        v = q * HALVES
        scale_own(q)
        gather_start(v)
        line_step(x_of(q + 1), 1)
        spectral_step(q + 1, 1, False)
        gather_near(v)
        for h in range(1, HALVES):
            gather_start(v + h)
        for k in range(2, time_count - 1):
            line_step(x_of(q + 1), k)
            spectral_step(q + 1, k, False)
        gather_far(v)

    after = {}

    def then(n, act, *args):
        after.setdefault(n, []).append(functools.partial(act, *args))

    def columns_bulk(v):
        @pl.loop(0, PIECES)
        def _(p):
            columns_start(v, p)

    unit = max(PIECES // 2, 1)
    for q in range(reps):
        first = q * HALVES * blocks
        if q + 1 < reps:
            then(first + blocks - 5 * unit, gather_near, q * HALVES + 1)
            for k in range(1, time_count - 1):
                then(first + blocks - 5 * unit, spectral_flush, q + 1, k)
            for k in range(max(2, time_count - 1), time_count):
                then(first + blocks - 2 * unit, line_step, x_of(q + 1), k)
                then(first + blocks - 2 * unit, spectral_step, q + 1, k)
        if q > 0:
            then(first - blocks + 3 * unit, scale_own, q)
            then(first - blocks + 3 * unit, gather_start, q * HALVES)
            then(first - 3 * unit, gather_near, q * HALVES)
            then(first - 1, gather_far, q * HALVES)
        for h in range(1, HALVES):
            v = q * HALVES + h
            if q > 0:
                then(first - 3 * unit, gather_start, v)
            if q > 0:
                then(v * blocks - 6 * unit, gather_near, v)
            then(v * blocks - 3 * unit, gather_far, v)
    for v in range(streams - 1):
        then(max((streams - 1) * blocks - 3 * unit, (v + 1) * blocks), columns_bulk, v)
    for v in range(streams - 1):
        then(total - 1 if v < streams - 2 else total + LAG * last - 2 * unit, columns_relay, v)

    @pl.loop(0, total + LAG * last)
    def _(n):
        v = lax.div(n, blocks)
        i = lax.rem(n, blocks)

        @pl.when((v < streams) & (i < time_count))
        def _():
            @pl.when(i == 0)
            def _():
                gather_finish(v)

            back(v, i)

        up_step(n)
        down_step(n)
        for at, acts in after.items():
            @pl.when(n == at)
            def _():
                for act in acts:
                    act()

    columns_relay(streams - 1)
    for v in range(streams):
        columns_finish(v)
        gather_drain(v)
    for q in range(reps):
        line_drain(x_of(q))
    line_drain(t_line)
    t_share_each(lambda copy: copy.wait_send())
    @pl.loop(0, time_count)
    def _(j):
        for d in range(pairs):
            pair_copy(reps - 1, j, d).wait_send()
            if d > 0:
                chip_copy(reps - 1, j, d).wait_send()

    @pl.loop(0, total)
    def _(n):
        row_copy(lax.div(n, blocks), lax.rem(n, blocks)).wait()

    for n in range(total - min(RING, total), total):
        q, m = n // blocks, n % blocks

        @pl.when(z < last)
        def _():
            up_copy(n, q, m).wait_send()

        @pl.when(z > 0)
        def _():
            down_copy(n, q, m).wait_send()


def solve_field(series, basis, tbasis, time_eig, space_eig, space_count, time_count):
    reps, time_local, rows = series.shape
    depth = basis.shape[1]
    times = tbasis.shape[1]
    own = depth // space_count
    pairs = space_count // 2
    blocks = PIECES * time_count
    block_rows = rows // blocks
    streams = reps * HALVES
    width = times // HALVES
    dma = pltpu.SemaphoreType.DMA
    hbm = pl.BlockSpec(memory_space=pl.ANY)
    vmem = pl.BlockSpec(memory_space=pltpu.VMEM)
    return pl.pallas_call(
        functools.partial(field_kernel, space_count, time_count),
        out_shape=(
            jax.ShapeDtypeStruct((blocks, block_rows, reps * times), BF16),
            jax.ShapeDtypeStruct((space_count, PIECES, block_rows, reps * times), BF16),
        ),
        in_specs=[hbm, hbm, hbm, vmem, vmem],
        out_specs=(hbm, hbm),
        scratch_shapes=[
            pltpu.VMEM((rows, depth), BF16),
            pltpu.VMEM((reps, time_count, time_local, rows), BF16),
            pltpu.VMEM((time_count, time_local, times), BF16),
            pltpu.VMEM((pairs, time_count, time_local, own), BF16),
            pltpu.VMEM((reps, pairs, time_count, time_local, own), BF16),
            pltpu.VMEM((pairs - 1, time_count, time_local, own), BF16),
            pltpu.VMEM((reps, pairs - 1, time_count, time_local, own), BF16),
            pltpu.VMEM((reps, time_count, time_local, own), F32),
            pltpu.VMEM((streams, width, depth), BF16),
            pltpu.VMEM((streams, blocks, block_rows, width), F32),
            pltpu.VMEM((streams, blocks, block_rows, width), BF16),
            pltpu.VMEM((streams, blocks, block_rows, width), BF16),
            pltpu.VMEM((RING, block_rows, width), BF16),
            pltpu.VMEM((RING, block_rows, width), BF16),
            dma((2 + reps,)),
            dma((reps, 2, time_count, PARTS)),
            dma((reps, time_count, PARTS)),
            dma((2, time_count)),
            dma((time_count,)),
            dma((2, pairs, time_count)),
            dma((pairs, time_count)),
            dma((reps, pairs, time_count)),
            dma((pairs - 1, time_count)),
            dma((reps, pairs - 1, time_count)),
            dma((streams, pairs - 1, 2)),
            dma((streams, space_count, 2)),
            dma((streams, pairs, 2)),
            dma((RING,)),
            dma((streams * blocks,)),
            dma((RING,)),
            dma((streams * blocks,)),
            dma((streams * blocks,)),
            dma((streams, PIECES, pairs)),
            dma((streams, space_count, PIECES)),
            dma((streams, PIECES, pairs)),
            dma((streams, PIECES)),
        ],
        compiler_params=pltpu.CompilerParams(
            collective_id=0, has_side_effects=True, vmem_limit_bytes=VMEM_BYTES
        ),
    )(series, basis, tbasis, time_eig, space_eig)


def grad_kernel(reps, wide, rows, columns, eig_ref, basis_ref, alpha_ref, grad_ref, alpha_scr, weighted, *halves):
    tile, blocks, sub = grad_ref.shape
    depth = rows.shape[1]
    times = depth // reps
    for q in range(reps):
        at = slice(q * times, (q + 1) * times)
        weighted[:, at] = (rows[:, at].astype(F32) * eig_ref[...] / depth).astype(BF16)
        alpha_scr[pl.ds(q, tile, stride=reps), :] = lax.dot_general(
            rows[:, at], basis_ref[...], CONTRACT_LAST, preferred_element_type=F32
        )
    alpha_ref[...] = alpha_scr[...].astype(BF16).reshape(alpha_ref.shape)
    for w in range(0, sub, wide):
        half = halves[w // wide % 2]
        for a in range(blocks):
            part = lax.dot_general(
                weighted[...], columns[a, w : w + wide, :], CONTRACT_LAST, preferred_element_type=F32
            )
            for v in range(0, wide, 128):
                half[v // 128, pl.ds(a, tile, stride=blocks), :] = part[:, v : v + 128]
        for v in range(0, wide, 128):
            grad_ref[:, :, w + v : w + v + 128] = half[v // 128].astype(BF16).reshape(tile, blocks, 128)


def grad_and_alpha(rows, columns, time_eig, time_basis, reps):
    row_count, depth = rows.shape
    blocks, sub, _ = columns.shape
    time_local, times = time_basis.shape
    tile = min(row_count, 256)
    wide = min(sub, 256)
    return pl.pallas_call(
        functools.partial(grad_kernel, reps, wide),
        out_shape=(
            jax.ShapeDtypeStruct((row_count, reps, time_local), BF16),
            jax.ShapeDtypeStruct((row_count, blocks, sub), BF16),
        ),
        grid=(row_count // tile,),
        in_specs=[
            pl.BlockSpec((tile, depth), lambda i: (i, 0)),
            pl.BlockSpec((blocks, sub, depth), lambda i: (0, 0, 0)),
            pl.BlockSpec((1, times), lambda i: (0, 0)),
            pl.BlockSpec((time_local, times), lambda i: (0, 0)),
        ],
        out_specs=(
            pl.BlockSpec((tile, reps, time_local), lambda i: (i, 0, 0)),
            pl.BlockSpec((tile, blocks, sub), lambda i: (i, 0, 0)),
        ),
        scratch_shapes=[
            pltpu.VMEM((tile * reps, time_local), F32),
            pltpu.VMEM((tile, depth), BF16),
            pltpu.VMEM((wide // 128, tile * blocks, 128), F32),
            pltpu.VMEM((wide // 128, tile * blocks, 128), F32),
        ],
    )(rows, columns, time_eig[None, :], time_basis)


def per_device(series, space_basis, time_basis, space_eig, time_eig):
    space_count = lax.axis_size("space")
    time_count = lax.axis_size("tm")
    rows, columns = solve_field(
        jnp.transpose(series, (1, 2, 0)),
        space_basis,
        time_basis,
        time_eig[None, :],
        space_eig[None, :],
        space_count,
        time_count,
    )
    depth = rows.shape[-1]
    return grad_and_alpha(
        rows.reshape(-1, depth), columns.reshape(space_count, -1, depth), time_eig, time_basis, series.shape[1]
    )


def solution(mesh):
    return jax.shard_map(
        per_device,
        mesh=mesh,
        in_specs=(P("space", None, "tm"), P("space", "tm"), P("tm", None), P(), P()),
        out_specs=(P("space", None, "tm"), P("space", None, "tm")),
        check_vma=False,
    )
```

```python
import functools

import jax
import jax.numpy as jnp
from jax import lax
from jax.experimental import pallas as pl
from jax.experimental.pallas import tpu as pltpu
from jax.sharding import PartitionSpec as P

F32 = jnp.float32
BF16 = jnp.bfloat16
MESH = pl.DeviceIdType.MESH
CONTRACT_LAST = (((1,), (1,)), ((), ()))
CONTRACT_FIRST = (((0,), (0,)), ((), ()))
VMEM_BYTES = 67043328
RING = 4
PIECES = 2
PARTS = 2
HALVES = 2
LAG = 2


def rcopy(src, dst, send_sem, recv_sem, **where):
    return pltpu.make_async_remote_copy(
        src_ref=src,
        dst_ref=dst,
        send_sem=send_sem,
        recv_sem=recv_sem,
        device_id=where,
        device_id_type=MESH,
    )


def field_kernel(
    space_count,
    time_count,
    series_hbm, basis_hbm, tbasis_hbm, time_eig_ref, space_eig_ref,
    rows_hbm, cols_hbm,
    basis, series, tbasis, pair_out, pair_in, chip_out, chip_in, mine, scaled, partial, below, above, up_out, down_out,
    load_sem, xs_sem, xr_sem, ts_sem, tr_sem, te_sem, ps_sem, pr_sem, cs_sem, cr_sem, gs_sem, gr_sem, fs_sem,
    us_sem, ur_sem, ds_sem, dr_sem, os_sem, ks_sem, kr_sem, kf_sem, ko_sem,
):
    reps, _, time_local, _ = series.shape
    streams, blocks, block_rows, width = partial.shape
    times = width * HALVES
    own = mine.shape[3]
    pairs = space_count // 2
    last = time_count - 1
    sub_rows = blocks * block_rows // time_count
    me = lax.axis_index("space")
    z = lax.axis_index("tm")
    core = lax.rem(me, 2)
    chip = lax.div(me, 2)
    partner = me + 1 - 2 * core
    total = streams * blocks

    def chip_at(d):
        return lax.bitwise_xor(chip, d)

    def peer(d):
        return 2 * chip_at(d) + core

    barrier = pltpu.get_barrier_semaphore()

    def greet(**where):
        pl.semaphore_signal(barrier, inc=1, device_id=where, device_id_type=MESH)

    @pl.when(z > 0)
    def _():
        greet(tm=z - 1)

    @pl.when(z < last)
    def _():
        greet(tm=z + 1)

    greet(space=partner)
    for d in range(1, pairs):
        greet(space=peer(d))

    loads = [pltpu.make_async_copy(series_hbm.at[q], series.at[q, z], load_sem.at[2 + q]) for q in range(reps)]
    for load in loads:
        load.start()
    share = time_local // pairs
    own_share = pl.ds(pl.multiple_of(chip * share, share), share)
    load_tbasis = pltpu.make_async_copy(tbasis_hbm.at[own_share], tbasis.at[z, own_share], load_sem.at[1])
    load_tbasis.start()
    load_basis = pltpu.make_async_copy(basis_hbm, basis, load_sem.at[0])

    @pl.when(z == 0)
    def _():
        below[...] = jnp.zeros_like(below)

    @pl.when(z == last)
    def _():
        above[...] = jnp.zeros_like(above)

    pl.semaphore_wait(barrier, pairs + jnp.minimum(z, 1) + jnp.minimum(last - z, 1))

    def x_copy(q, j, way, step, p):
        size = time_local // PARTS
        at = series.at[q, j, pl.ds(p * size, size)]
        return rcopy(at, at, xs_sem.at[q, way, step, p], xr_sem.at[q, j, p], tm=z + 1 - 2 * way)

    def t_copy(j, way, step, p):
        at = tbasis.at[j, own_share]
        return rcopy(at, at, ts_sem.at[way, step], tr_sem.at[j], tm=z + 1 - 2 * way)

    def t_share(j, d):
        at = tbasis.at[j, own_share]
        return rcopy(at, at, te_sem.at[0, d, j], te_sem.at[1, d, j], space=peer(d))

    def t_share_step(k):
        @pl.loop(0, 1 if k == 0 else 2)
        def _(side):
            j = z + k * (2 * side - 1)

            @pl.when((j >= 0) & (j <= last))
            def _():
                for d in range(1, pairs):
                    t_share(j, d).start()

    def t_share_each(act):
        @pl.loop(0, time_count)
        def _(j):
            for d in range(1, pairs):
                act(t_share(j, d))

    def line_start(line):
        copy, parts = line
        for p in range(parts):
            @pl.when(z < last)
            def _():
                copy(z, 0, 0, p).start()

            @pl.when(z > 0)
            def _():
                copy(z, 1, 0, p).start()

    def line_part(line, k, p):
        copy, _ = line

        @pl.when(z >= k)
        def _():
            copy(z - k, 0, k, p).wait_recv()

            @pl.when(z < last)
            def _():
                copy(z - k, 0, k, p).start()

        @pl.when(z + k <= last)
        def _():
            copy(z + k, 1, k, p).wait_recv()

            @pl.when(z > 0)
            def _():
                copy(z + k, 1, k, p).start()

    def line_step(line, k):
        for p in range(line[1]):
            line_part(line, k, p)

    def line_drain(line):
        copy, parts = line
        for k in range(time_count):
            for p in range(parts):
                @pl.when((z >= k) & (z < last))
                def _():
                    copy(z - k, 0, k, p).wait_send()

                @pl.when((z + k <= last) & (z > 0))
                def _():
                    copy(z + k, 1, k, p).wait_send()

    def x_of(q):
        return functools.partial(x_copy, q), PARTS

    t_line = t_copy, 1

    def pair_copy(q, j, d):
        return rcopy(pair_out.at[d, j], pair_in.at[q, d, j], ps_sem.at[d, j], pr_sem.at[q, d, j], space=partner)

    def chip_copy(q, j, d):
        return rcopy(
            chip_out.at[d - 1, j], chip_in.at[q, d - 1, j], cs_sem.at[d - 1, j], cr_sem.at[q, d - 1, j], space=peer(d)
        )

    def spectrum(q, j, c):
        at = pl.ds(pl.multiple_of(c * own, own), own)
        return jnp.dot(series[q, j], basis[:, at], preferred_element_type=F32)

    def spectral(q, j, send=True):
        @pl.loop(0, pairs + 2)
        def _(n):
            @pl.when(n < pairs)
            def _():
                d = pairs - 1 - n
                if q > 0:
                    pair_copy(q - 1, j, d).wait_send()
                pair_out[d, j] = spectrum(q, j, 2 * chip_at(d) + 1 - core).astype(BF16)
                pair_copy(q, j, d).start()

            @pl.when(n >= 2)
            def _():
                d = pairs + 1 - n
                value = spectrum(q, j, peer(d))
                pair_copy(q, j, d).wait_recv()
                value = value + pair_in[q, d, j].astype(F32)

                @pl.when(d > 0)
                def _():
                    if q > 0:
                        chip_copy(q - 1, j, d).wait_send()
                    chip_out[d - 1, j] = value.astype(BF16)
                    if send:
                        chip_copy(q, j, d).start()

                @pl.when(d == 0)
                def _():
                    mine[q, j] = value

    def spectral_side(q, k, side):
        j = jnp.where(2 * z < time_count, z + k * (1 - 2 * side), z + k * (2 * side - 1))

        @pl.when((j >= 0) & (j <= last))
        def _():
            spectral(q, j)

    def spectral_step(q, k, send=True):
        @pl.loop(0, 2)
        def _(side):
            j = z + k * (2 * side - 1)

            @pl.when((j >= 0) & (j <= last))
            def _():
                spectral(q, j, send)

    def spectral_flush(q, k):
        @pl.loop(0, 2)
        def _(side):
            j = z + k * (2 * side - 1)

            @pl.when((j >= 0) & (j <= last))
            def _():
                for d in reversed(range(1, pairs)):
                    chip_copy(q, j, d).start()

    bits = [1 << b for b in range(pairs.bit_length() - 1)]
    near = [d for d in range(1, pairs) if d in bits]
    turns = [(e, f) for e in bits for f in bits if e != f]
    far = [d for d in range(1, pairs) if d not in bits]
    direct = [d for d in far if d not in [e ^ f for e, f in turns]]

    def piece(v, j, g):
        rows = pl.ds(g * (width // 2), width // 2)
        return scaled.at[v, rows, pl.ds(pl.multiple_of(j * own, own), own)]

    def gather_copy(v, d, g):
        return rcopy(
            piece(v, me, g), piece(v, me, g), gs_sem.at[v, d - 1, g], gr_sem.at[v, me, g], space=peer(d)
        )

    def turn_copy(v, e, f):
        g = 0 if e < f else 1
        at = piece(v, peer(e), g)
        return rcopy(at, at, gs_sem.at[v, (e ^ f) - 1, g], gr_sem.at[v, peer(e), g], space=peer(f))

    def forward_copy(v, j, d, g):
        return rcopy(piece(v, j, g), piece(v, j, g), fs_sem.at[v, d, g], gr_sem.at[v, j, g], space=partner)

    def scale_own(q):
        @pl.loop(0, time_count)
        def _(j):
            for d in range(1, pairs):
                chip_copy(q, j, d).wait_recv()

        value = mine[q]
        for d in range(1, pairs):
            value = value + chip_in[q, d - 1].astype(F32)
        value = value.reshape(time_count * time_local, own)
        rotation = tbasis[...].reshape(time_count * time_local, times)
        turned = lax.dot_general(rotation, value.astype(BF16), CONTRACT_FIRST, preferred_element_type=F32)
        times_eig = jnp.transpose(jnp.broadcast_to(time_eig_ref[...], (8, times)))[:, :1]
        first = pl.multiple_of((z * space_count + me) * own, own)
        turned = turned / (times_eig * space_eig_ref[:, pl.ds(first, own)] + 0.1)
        for h in range(HALVES):
            scaled[q * HALVES + h, :, pl.ds(pl.multiple_of(me * own, own), own)] = turned[
                h * width : (h + 1) * width
            ].astype(BF16)

    def gather_start(v):
        for g in range(2):
            for d in near + direct:
                gather_copy(v, d, g).start()
            forward_copy(v, me, 0, g).start()

    def gather_near(v):
        for g in range(2):
            for e in near:
                forward_copy(v, peer(e), e, g).wait_recv()
                for f in near:
                    if f != e and g == (0 if e < f else 1):
                        turn_copy(v, e, f).start()
                forward_copy(v, peer(e), e, g).start()

    def gather_far(v):
        for g in range(2):
            for d in far:
                forward_copy(v, peer(d), d, g).wait_recv()
                forward_copy(v, peer(d), d, g).start()

    def gather_finish(v):
        for d in range(pairs):
            for g in range(2):
                forward_copy(v, peer(d) + 1 - 2 * core, d, g).wait_recv()

    def gather_drain(v):
        for g in range(2):
            for d in near + direct:
                gather_copy(v, d, g).wait_send()
            for d in range(pairs):
                forward_copy(v, peer(d), d, g).wait_send()
        for e, f in turns:
            turn_copy(v, e, f).wait_send()

    def back(q, i):
        low = lax.div(i, 2)
        side = lax.rem(i, 2)
        side = jnp.where(2 * z < time_count, side, 1 - side)
        sub = jnp.where(side == 0, last - low, low)
        value = lax.dot_general(
            basis[pl.ds(pl.multiple_of(sub * sub_rows, sub_rows), sub_rows), :],
            scaled[q],
            CONTRACT_LAST,
            preferred_element_type=F32,
        )
        partial[q, pl.ds(sub * PIECES, PIECES)] = value.reshape(PIECES, block_rows, width)

    def up_copy(n, q, m):
        slot = lax.rem(n, RING)
        return rcopy(up_out.at[slot], below.at[q, m], us_sem.at[slot], ur_sem.at[n], tm=z + 1)

    def down_copy(n, q, m):
        slot = lax.rem(n, RING)
        return rcopy(down_out.at[slot], above.at[q, m], ds_sem.at[slot], dr_sem.at[n], tm=z - 1)

    def rep_columns(q):
        return pl.ds(pl.multiple_of(q * width, width), width)

    def row_copy(q, m):
        return pltpu.make_async_copy(below.at[q, m], rows_hbm.at[m, :, rep_columns(q)], os_sem.at[q * blocks + m])

    def column_at(q, p, j):
        return cols_hbm.at[j, p, :, rep_columns(q)]

    def column_copy(q, p, d):
        source = below.at[q, z * PIECES + p]
        return rcopy(source, column_at(q, p, me), ks_sem.at[q, p, d], kr_sem.at[q, me, p], space=peer(d))

    def column_pair(q, p):
        source = below.at[q, z * PIECES + p]
        return rcopy(source, column_at(q, p, me), kf_sem.at[q, p, 0], kr_sem.at[q, me, p], space=partner)

    def column_own(q, p):
        return pltpu.make_async_copy(below.at[q, z * PIECES + p], column_at(q, p, me), ko_sem.at[q, p])

    def column_forward(q, p, j, d):
        at = column_at(q, p, j)
        return rcopy(at, at, kf_sem.at[q, p, d], kr_sem.at[q, j, p], space=partner)

    def columns_start(q, p):
        for d in reversed(range(1, pairs)):
            column_copy(q, p, d).start()
        column_pair(q, p).start()
        column_own(q, p).start()

    def columns_relay(q):
        @pl.loop(0, PIECES)
        def _(n):
            p = jnp.where(2 * z < time_count, PIECES - 1 - n, n)
            p = jnp.where((z == 0) | (z == last), PIECES - 1 - p, p)
            for d in range(1, pairs):
                column_forward(q, p, peer(d), d).wait_recv()
                column_forward(q, p, peer(d), d).start()

    def columns_finish(q):
        @pl.loop(0, PIECES)
        def _(p):
            for d in range(pairs):
                column_forward(q, p, peer(d) + 1 - 2 * core, d).wait_recv()
            for d in range(1, pairs):
                column_copy(q, p, d).wait_send()
                column_forward(q, p, peer(d), d).wait_send()
            column_pair(q, p).wait_send()
            column_own(q, p).wait()

    def finish_block(q, m):
        below[q, m] = (partial[q, m] + below[q, m].astype(F32) + above[q, m].astype(F32)).astype(BF16)
        row_copy(q, m).start()

        @pl.when((lax.div(m, PIECES) == z) & (q == streams - 1))
        def _():
            columns_start(q, lax.rem(m, PIECES))

    def up_step(n):
        at = n - LAG * z

        @pl.when((at >= 0) & (at < total))
        def _():
            q = lax.div(at, blocks)
            m = blocks - 1 - lax.rem(at, blocks)

            @pl.when(z > 0)
            def _():
                up_copy(at, q, m).wait_recv()

            @pl.when(z < last)
            def _():
                @pl.when(at >= RING)
                def _():
                    up_copy(at, q, m).wait_send()

                @pl.when(z == 0)
                def _():
                    up_out[lax.rem(at, RING)] = partial[q, m].astype(BF16)

                @pl.when(z > 0)
                def _():
                    up_out[lax.rem(at, RING)] = (partial[q, m] + below[q, m].astype(F32)).astype(BF16)

                up_copy(at, q, m).start()

            @pl.when((z == last) | ((z > 0) & (q * blocks + m + LAG * (last - z) < n)))
            def _():
                finish_block(q, m)

    def down_step(n):
        at = n - LAG * (last - z)

        @pl.when((at >= 0) & (at < total))
        def _():
            q = lax.div(at, blocks)
            m = lax.rem(at, blocks)

            @pl.when(z < last)
            def _():
                down_copy(at, q, m).wait_recv()

            @pl.when(z > 0)
            def _():
                @pl.when(at >= RING)
                def _():
                    down_copy(at, q, m).wait_send()

                @pl.when(z == last)
                def _():
                    down_out[lax.rem(at, RING)] = partial[q, m].astype(BF16)

                @pl.when(z < last)
                def _():
                    down_out[lax.rem(at, RING)] = (partial[q, m] + above[q, m].astype(F32)).astype(BF16)

                down_copy(at, q, m).start()

            @pl.when((z == 0) | ((z < last) & (q * blocks + blocks - 1 - m + LAG * z <= n)))
            def _():
                finish_block(q, m)

    for load in loads:
        load.wait()
    line_start(x_of(0))
    load_basis.start()
    load_tbasis.wait()
    line_start(t_line)
    t_share_step(0)
    load_basis.wait()
    spectral(0, z)
    work = [functools.partial(spectral, q, z) for q in range(1, reps)]
    for k in range(1, time_count):
        for p in range(PARTS):
            if work and k > 1:
                work.pop(0)()
            if p == 0 and k == max(1, time_count - 1):
                for q in range(1, reps):
                    line_start(x_of(q))
            line_part(x_of(0), k, p)
            if p == PARTS - 1:
                line_step(t_line, k)
                t_share_step(k)
            if work and k == 1:
                work.pop(0)()
        while work:
            work.pop(0)()
        work = [functools.partial(spectral_side, 0, k, side) for side in range(2)]
    while work:
        work.pop(0)()
    for q in range(reps - 1):
        if q == 0:
            t_share_each(lambda copy: copy.wait_recv())
        v = q * HALVES
        scale_own(q)
        gather_start(v)
        line_step(x_of(q + 1), 1)
        spectral_step(q + 1, 1, False)
        gather_near(v)
        for h in range(1, HALVES):
            gather_start(v + h)

        @pl.when((z > 0) & (z < last))
        def _():
            for k in range(2, time_count - 1):
                line_step(x_of(q + 1), k)
                spectral_step(q + 1, k, False)

        gather_far(v)

    after = {}

    def then(n, act, *args):
        after.setdefault(n, []).append(functools.partial(act, *args))

    def slices_flush(q):
        spectral_flush(q, 1)

        @pl.when((z > 0) & (z < last))
        def _():
            for k in range(2, time_count - 1):
                spectral_flush(q, k)

    def slices_of_ends(q):
        @pl.when((z == 0) | (z == last))
        def _():
            for k in range(2, time_count - 1):
                line_step(x_of(q), k)
                spectral_step(q, k)

    def columns_bulk(v):
        @pl.loop(0, PIECES)
        def _(p):
            columns_start(v, p)

    unit = max(PIECES // 2, 1)
    for q in range(reps):
        first = q * HALVES * blocks
        if q + 1 < reps:
            then(first + blocks - 5 * unit, gather_near, q * HALVES + 1)
            then(first + blocks - 5 * unit, slices_flush, q + 1)
            then(first + blocks - 4 * unit, slices_of_ends, q + 1)
            for k in range(max(2, time_count - 1), time_count):
                then(first + blocks - 2 * unit, line_step, x_of(q + 1), k)
                then(first + blocks - 2 * unit, spectral_step, q + 1, k)
        if q > 0:
            then(first - blocks + 3 * unit, scale_own, q)
            then(first - blocks + 3 * unit, gather_start, q * HALVES)
            then(first - 3 * unit, gather_near, q * HALVES)
            then(first - 1, gather_far, q * HALVES)
        for h in range(1, HALVES):
            v = q * HALVES + h
            if q > 0:
                then(first - 3 * unit, gather_start, v)
            if q > 0:
                then(v * blocks - 6 * unit, gather_near, v)
            then(v * blocks - 3 * unit, gather_far, v)
    for v in range(streams - 1):
        then(max((streams - 1) * blocks - 3 * unit, (v + 1) * blocks), columns_bulk, v)
    for v in range(streams - 1):
        then(total - 1 if v < streams - 2 else total + LAG * last - 2 * unit, columns_relay, v)

    @pl.loop(0, total + LAG * last)
    def _(n):
        v = lax.div(n, blocks)
        i = lax.rem(n, blocks)

        @pl.when((v < streams) & (i < time_count))
        def _():
            @pl.when(i == 0)
            def _():
                gather_finish(v)

            back(v, i)

        up_step(n)
        down_step(n)
        for at, acts in after.items():
            @pl.when(n == at)
            def _():
                for act in acts:
                    act()

    columns_relay(streams - 1)
    for v in range(streams):
        columns_finish(v)
        gather_drain(v)
    for q in range(reps):
        line_drain(x_of(q))
    line_drain(t_line)
    t_share_each(lambda copy: copy.wait_send())
    @pl.loop(0, time_count)
    def _(j):
        for d in range(pairs):
            pair_copy(reps - 1, j, d).wait_send()
            if d > 0:
                chip_copy(reps - 1, j, d).wait_send()

    @pl.loop(0, total)
    def _(n):
        row_copy(lax.div(n, blocks), lax.rem(n, blocks)).wait()

    for n in range(total - min(RING, total), total):
        q, m = n // blocks, n % blocks

        @pl.when(z < last)
        def _():
            up_copy(n, q, m).wait_send()

        @pl.when(z > 0)
        def _():
            down_copy(n, q, m).wait_send()


def solve_field(series, basis, tbasis, time_eig, space_eig, space_count, time_count):
    reps, time_local, rows = series.shape
    depth = basis.shape[1]
    times = tbasis.shape[1]
    own = depth // space_count
    pairs = space_count // 2
    blocks = PIECES * time_count
    block_rows = rows // blocks
    streams = reps * HALVES
    width = times // HALVES
    dma = pltpu.SemaphoreType.DMA
    hbm = pl.BlockSpec(memory_space=pl.ANY)
    vmem = pl.BlockSpec(memory_space=pltpu.VMEM)
    return pl.pallas_call(
        functools.partial(field_kernel, space_count, time_count),
        out_shape=(
            jax.ShapeDtypeStruct((blocks, block_rows, reps * times), BF16),
            jax.ShapeDtypeStruct((space_count, PIECES, block_rows, reps * times), BF16),
        ),
        in_specs=[hbm, hbm, hbm, vmem, vmem],
        out_specs=(hbm, hbm),
        scratch_shapes=[
            pltpu.VMEM((rows, depth), BF16),
            pltpu.VMEM((reps, time_count, time_local, rows), BF16),
            pltpu.VMEM((time_count, time_local, times), BF16),
            pltpu.VMEM((pairs, time_count, time_local, own), BF16),
            pltpu.VMEM((reps, pairs, time_count, time_local, own), BF16),
            pltpu.VMEM((pairs - 1, time_count, time_local, own), BF16),
            pltpu.VMEM((reps, pairs - 1, time_count, time_local, own), BF16),
            pltpu.VMEM((reps, time_count, time_local, own), F32),
            pltpu.VMEM((streams, width, depth), BF16),
            pltpu.VMEM((streams, blocks, block_rows, width), F32),
            pltpu.VMEM((streams, blocks, block_rows, width), BF16),
            pltpu.VMEM((streams, blocks, block_rows, width), BF16),
            pltpu.VMEM((RING, block_rows, width), BF16),
            pltpu.VMEM((RING, block_rows, width), BF16),
            dma((2 + reps,)),
            dma((reps, 2, time_count, PARTS)),
            dma((reps, time_count, PARTS)),
            dma((2, time_count)),
            dma((time_count,)),
            dma((2, pairs, time_count)),
            dma((pairs, time_count)),
            dma((reps, pairs, time_count)),
            dma((pairs - 1, time_count)),
            dma((reps, pairs - 1, time_count)),
            dma((streams, pairs - 1, 2)),
            dma((streams, space_count, 2)),
            dma((streams, pairs, 2)),
            dma((RING,)),
            dma((streams * blocks,)),
            dma((RING,)),
            dma((streams * blocks,)),
            dma((streams * blocks,)),
            dma((streams, PIECES, pairs)),
            dma((streams, space_count, PIECES)),
            dma((streams, PIECES, pairs)),
            dma((streams, PIECES)),
        ],
        compiler_params=pltpu.CompilerParams(
            collective_id=0, has_side_effects=True, vmem_limit_bytes=VMEM_BYTES
        ),
    )(series, basis, tbasis, time_eig, space_eig)


def grad_kernel(reps, wide, rows, columns, eig_ref, basis_ref, alpha_ref, grad_ref, alpha_scr, weighted, *halves):
    tile, blocks, sub = grad_ref.shape
    depth = rows.shape[1]
    times = depth // reps
    for q in range(reps):
        at = slice(q * times, (q + 1) * times)
        weighted[:, at] = (rows[:, at].astype(F32) * eig_ref[...] / depth).astype(BF16)
        alpha_scr[pl.ds(q, tile, stride=reps), :] = lax.dot_general(
            rows[:, at], basis_ref[...], CONTRACT_LAST, preferred_element_type=F32
        )
    alpha_ref[...] = alpha_scr[...].astype(BF16).reshape(alpha_ref.shape)
    for w in range(0, sub, wide):
        half = halves[w // wide % 2]
        for a in range(blocks):
            part = lax.dot_general(
                weighted[...], columns[a, w : w + wide, :], CONTRACT_LAST, preferred_element_type=F32
            )
            for v in range(0, wide, 128):
                half[v // 128, pl.ds(a, tile, stride=blocks), :] = part[:, v : v + 128]
        for v in range(0, wide, 128):
            grad_ref[:, :, w + v : w + v + 128] = half[v // 128].astype(BF16).reshape(tile, blocks, 128)


def grad_and_alpha(rows, columns, time_eig, time_basis, reps):
    row_count, depth = rows.shape
    blocks, sub, _ = columns.shape
    time_local, times = time_basis.shape
    tile = min(row_count, 256)
    wide = min(sub, 256)
    return pl.pallas_call(
        functools.partial(grad_kernel, reps, wide),
        out_shape=(
            jax.ShapeDtypeStruct((row_count, reps, time_local), BF16),
            jax.ShapeDtypeStruct((row_count, blocks, sub), BF16),
        ),
        grid=(row_count // tile,),
        in_specs=[
            pl.BlockSpec((tile, depth), lambda i: (i, 0)),
            pl.BlockSpec((blocks, sub, depth), lambda i: (0, 0, 0)),
            pl.BlockSpec((1, times), lambda i: (0, 0)),
            pl.BlockSpec((time_local, times), lambda i: (0, 0)),
        ],
        out_specs=(
            pl.BlockSpec((tile, reps, time_local), lambda i: (i, 0, 0)),
            pl.BlockSpec((tile, blocks, sub), lambda i: (i, 0, 0)),
        ),
        scratch_shapes=[
            pltpu.VMEM((tile * reps, time_local), F32),
            pltpu.VMEM((tile, depth), BF16),
            pltpu.VMEM((wide // 128, tile * blocks, 128), F32),
            pltpu.VMEM((wide // 128, tile * blocks, 128), F32),
        ],
    )(rows, columns, time_eig[None, :], time_basis)


def per_device(series, space_basis, time_basis, space_eig, time_eig):
    space_count = lax.axis_size("space")
    time_count = lax.axis_size("tm")
    rows, columns = solve_field(
        jnp.transpose(series, (1, 2, 0)),
        space_basis,
        time_basis,
        time_eig[None, :],
        space_eig[None, :],
        space_count,
        time_count,
    )
    depth = rows.shape[-1]
    return grad_and_alpha(
        rows.reshape(-1, depth), columns.reshape(space_count, -1, depth), time_eig, time_basis, series.shape[1]
    )


def solution(mesh):
    return jax.shard_map(
        per_device,
        mesh=mesh,
        in_specs=(P("space", None, "tm"), P("space", "tm"), P("tm", None), P(), P()),
        out_specs=(P("space", None, "tm"), P("space", None, "tm")),
        check_vma=False,
    )
```

```python
import functools

import jax
import jax.numpy as jnp
from jax import lax
from jax.experimental import pallas as pl
from jax.experimental.pallas import tpu as pltpu
from jax.sharding import PartitionSpec as P

F32 = jnp.float32
BF16 = jnp.bfloat16
MESH = pl.DeviceIdType.MESH
CONTRACT_LAST = (((1,), (1,)), ((), ()))
CONTRACT_FIRST = (((0,), (0,)), ((), ()))
VMEM_BYTES = 67043328
RING = 4
PIECES = 2
PARTS = 2
HALVES = 2
LAG = 2


def rcopy(src, dst, send_sem, recv_sem, **where):
    return pltpu.make_async_remote_copy(
        src_ref=src,
        dst_ref=dst,
        send_sem=send_sem,
        recv_sem=recv_sem,
        device_id=where,
        device_id_type=MESH,
    )


def field_kernel(
    space_count,
    time_count,
    series_hbm, basis_hbm, tbasis_hbm, time_eig_ref, space_eig_ref,
    rows_hbm, cols_hbm,
    basis, series, tbasis, pair_out, pair_in, chip_out, chip_in, mine, scaled, partial, below, above, up_out, down_out,
    load_sem, xs_sem, xr_sem, ts_sem, tr_sem, te_sem, ps_sem, pr_sem, cs_sem, cr_sem, gs_sem, gr_sem, fs_sem,
    us_sem, ur_sem, ds_sem, dr_sem, os_sem, ks_sem, kr_sem, kf_sem, ko_sem,
):
    reps, _, time_local, _ = series.shape
    streams, blocks, block_rows, width = partial.shape
    times = width * HALVES
    own = mine.shape[3]
    pairs = space_count // 2
    last = time_count - 1
    sub_rows = blocks * block_rows // time_count
    me = lax.axis_index("space")
    z = lax.axis_index("tm")
    core = lax.rem(me, 2)
    chip = lax.div(me, 2)
    partner = me + 1 - 2 * core
    total = streams * blocks

    def chip_at(d):
        return lax.bitwise_xor(chip, d)

    def peer(d):
        return 2 * chip_at(d) + core

    barrier = pltpu.get_barrier_semaphore()

    def greet(**where):
        pl.semaphore_signal(barrier, inc=1, device_id=where, device_id_type=MESH)

    @pl.when(z > 0)
    def _():
        greet(tm=z - 1)

    @pl.when(z < last)
    def _():
        greet(tm=z + 1)

    greet(space=partner)
    for d in range(1, pairs):
        greet(space=peer(d))

    loads = [pltpu.make_async_copy(series_hbm.at[q], series.at[q, z], load_sem.at[2 + q]) for q in range(reps)]
    for load in loads:
        load.start()
    share = time_local // pairs
    own_share = pl.ds(pl.multiple_of(chip * share, share), share)
    load_tbasis = pltpu.make_async_copy(tbasis_hbm.at[own_share], tbasis.at[z, own_share], load_sem.at[1])
    load_tbasis.start()
    load_basis = pltpu.make_async_copy(basis_hbm, basis, load_sem.at[0])

    @pl.when(z == 0)
    def _():
        below[...] = jnp.zeros_like(below)

    @pl.when(z == last)
    def _():
        above[...] = jnp.zeros_like(above)

    pl.semaphore_wait(barrier, pairs + jnp.minimum(z, 1) + jnp.minimum(last - z, 1))

    def x_copy(q, j, way, step, p):
        size = time_local // PARTS
        at = series.at[q, j, pl.ds(p * size, size)]
        return rcopy(at, at, xs_sem.at[q, way, step, p], xr_sem.at[q, j, p], tm=z + 1 - 2 * way)

    def t_copy(j, way, step, p):
        at = tbasis.at[j, own_share]
        return rcopy(at, at, ts_sem.at[way, step], tr_sem.at[j], tm=z + 1 - 2 * way)

    def t_share(j, d):
        at = tbasis.at[j, own_share]
        return rcopy(at, at, te_sem.at[0, d, j], te_sem.at[1, d, j], space=peer(d))

    def t_share_step(k):
        @pl.loop(0, 1 if k == 0 else 2)
        def _(side):
            j = z + k * (2 * side - 1)

            @pl.when((j >= 0) & (j <= last))
            def _():
                for d in range(1, pairs):
                    t_share(j, d).start()

    def t_share_each(act):
        @pl.loop(0, time_count)
        def _(j):
            for d in range(1, pairs):
                act(t_share(j, d))

    def line_start(line):
        copy, parts = line
        for p in range(parts):
            @pl.when(z < last)
            def _():
                copy(z, 0, 0, p).start()

            @pl.when(z > 0)
            def _():
                copy(z, 1, 0, p).start()

    def line_part(line, k, p):
        copy, _ = line

        @pl.when(z >= k)
        def _():
            copy(z - k, 0, k, p).wait_recv()

            @pl.when(z < last)
            def _():
                copy(z - k, 0, k, p).start()

        @pl.when(z + k <= last)
        def _():
            copy(z + k, 1, k, p).wait_recv()

            @pl.when(z > 0)
            def _():
                copy(z + k, 1, k, p).start()

    def line_step(line, k):
        for p in range(line[1]):
            line_part(line, k, p)

    def line_drain(line):
        copy, parts = line
        for k in range(time_count):
            for p in range(parts):
                @pl.when((z >= k) & (z < last))
                def _():
                    copy(z - k, 0, k, p).wait_send()

                @pl.when((z + k <= last) & (z > 0))
                def _():
                    copy(z + k, 1, k, p).wait_send()

    def x_of(q):
        return functools.partial(x_copy, q), PARTS

    t_line = t_copy, 1

    def pair_copy(q, j, d):
        return rcopy(pair_out.at[d, j], pair_in.at[q, d, j], ps_sem.at[d, j], pr_sem.at[q, d, j], space=partner)

    def chip_copy(q, j, d):
        return rcopy(
            chip_out.at[d - 1, j], chip_in.at[q, d - 1, j], cs_sem.at[d - 1, j], cr_sem.at[q, d - 1, j], space=peer(d)
        )

    def spectrum(q, j, c):
        at = pl.ds(pl.multiple_of(c * own, own), own)
        return jnp.dot(series[q, j], basis[:, at], preferred_element_type=F32)

    def spectral(q, j, send=True):
        @pl.loop(0, pairs + 2)
        def _(n):
            @pl.when(n < pairs)
            def _():
                d = pairs - 1 - n
                if q > 0:
                    pair_copy(q - 1, j, d).wait_send()
                pair_out[d, j] = spectrum(q, j, 2 * chip_at(d) + 1 - core).astype(BF16)
                pair_copy(q, j, d).start()

            @pl.when(n >= 2)
            def _():
                d = pairs + 1 - n
                value = spectrum(q, j, peer(d))
                pair_copy(q, j, d).wait_recv()
                value = value + pair_in[q, d, j].astype(F32)

                @pl.when(d > 0)
                def _():
                    if q > 0:
                        chip_copy(q - 1, j, d).wait_send()
                    chip_out[d - 1, j] = value.astype(BF16)
                    if send:
                        chip_copy(q, j, d).start()

                @pl.when(d == 0)
                def _():
                    mine[q, j] = value

    def spectral_side(q, k, side):
        j = jnp.where(2 * z < time_count, z + k * (1 - 2 * side), z + k * (2 * side - 1))

        @pl.when((j >= 0) & (j <= last))
        def _():
            spectral(q, j)

    def spectral_step(q, k, send=True):
        @pl.loop(0, 2)
        def _(side):
            j = z + k * (2 * side - 1)

            @pl.when((j >= 0) & (j <= last))
            def _():
                spectral(q, j, send)

    def spectral_flush(q, k):
        @pl.loop(0, 2)
        def _(side):
            j = z + k * (2 * side - 1)

            @pl.when((j >= 0) & (j <= last))
            def _():
                for d in reversed(range(1, pairs)):
                    chip_copy(q, j, d).start()

    bits = [1 << b for b in range(pairs.bit_length() - 1)]
    near = [d for d in range(1, pairs) if d in bits]
    turns = [(e, f) for e in bits for f in bits if e != f]
    far = [d for d in range(1, pairs) if d not in bits]
    direct = [d for d in far if d not in [e ^ f for e, f in turns]]

    def piece(v, j, g):
        rows = pl.ds(g * (width // 2), width // 2)
        return scaled.at[v, rows, pl.ds(pl.multiple_of(j * own, own), own)]

    def gather_copy(v, d, g):
        return rcopy(
            piece(v, me, g), piece(v, me, g), gs_sem.at[v, d - 1, g], gr_sem.at[v, me, g], space=peer(d)
        )

    def turn_copy(v, e, f):
        g = 0 if e < f else 1
        at = piece(v, peer(e), g)
        return rcopy(at, at, gs_sem.at[v, (e ^ f) - 1, g], gr_sem.at[v, peer(e), g], space=peer(f))

    def forward_copy(v, j, d, g):
        return rcopy(piece(v, j, g), piece(v, j, g), fs_sem.at[v, d, g], gr_sem.at[v, j, g], space=partner)

    def scale_own(q):
        @pl.loop(0, time_count)
        def _(j):
            for d in range(1, pairs):
                chip_copy(q, j, d).wait_recv()

        value = mine[q]
        for d in range(1, pairs):
            value = value + chip_in[q, d - 1].astype(F32)
        value = value.reshape(time_count * time_local, own)
        rotation = tbasis[...].reshape(time_count * time_local, times)
        turned = lax.dot_general(rotation, value.astype(BF16), CONTRACT_FIRST, preferred_element_type=F32)
        times_eig = jnp.transpose(jnp.broadcast_to(time_eig_ref[...], (8, times)))[:, :1]
        first = pl.multiple_of((z * space_count + me) * own, own)
        turned = turned / (times_eig * space_eig_ref[:, pl.ds(first, own)] + 0.1)
        for h in range(HALVES):
            scaled[q * HALVES + h, :, pl.ds(pl.multiple_of(me * own, own), own)] = turned[
                h * width : (h + 1) * width
            ].astype(BF16)

    def gather_start(v):
        for g in range(2):
            for d in near + direct:
                gather_copy(v, d, g).start()
            forward_copy(v, me, 0, g).start()

    def gather_near(v):
        for g in range(2):
            for e in near:
                forward_copy(v, peer(e), e, g).wait_recv()
                for f in near:
                    if f != e and g == (0 if e < f else 1):
                        turn_copy(v, e, f).start()
                forward_copy(v, peer(e), e, g).start()

    def gather_far(v):
        for g in range(2):
            for d in far:
                forward_copy(v, peer(d), d, g).wait_recv()
                forward_copy(v, peer(d), d, g).start()

    def gather_finish(v):
        for d in range(pairs):
            for g in range(2):
                forward_copy(v, peer(d) + 1 - 2 * core, d, g).wait_recv()

    def gather_drain(v):
        for g in range(2):
            for d in near + direct:
                gather_copy(v, d, g).wait_send()
            for d in range(pairs):
                forward_copy(v, peer(d), d, g).wait_send()
        for e, f in turns:
            turn_copy(v, e, f).wait_send()

    def back(q, i):
        low = lax.div(i, 2)
        side = lax.rem(i, 2)
        side = jnp.where(2 * z < time_count, side, 1 - side)
        sub = jnp.where(side == 0, last - low, low)
        value = lax.dot_general(
            basis[pl.ds(pl.multiple_of(sub * sub_rows, sub_rows), sub_rows), :],
            scaled[q],
            CONTRACT_LAST,
            preferred_element_type=F32,
        )
        partial[q, pl.ds(sub * PIECES, PIECES)] = value.reshape(PIECES, block_rows, width)

    def up_copy(n, q, m):
        slot = lax.rem(n, RING)
        return rcopy(up_out.at[slot], below.at[q, m], us_sem.at[slot], ur_sem.at[n], tm=z + 1)

    def down_copy(n, q, m):
        slot = lax.rem(n, RING)
        return rcopy(down_out.at[slot], above.at[q, m], ds_sem.at[slot], dr_sem.at[n], tm=z - 1)

    def rep_columns(q):
        return pl.ds(pl.multiple_of(q * width, width), width)

    def row_copy(q, m):
        return pltpu.make_async_copy(below.at[q, m], rows_hbm.at[m, :, rep_columns(q)], os_sem.at[q * blocks + m])

    def column_at(q, p, j):
        return cols_hbm.at[j, p, :, rep_columns(q)]

    def column_copy(q, p, d):
        source = below.at[q, z * PIECES + p]
        return rcopy(source, column_at(q, p, me), ks_sem.at[q, p, d], kr_sem.at[q, me, p], space=peer(d))

    def column_pair(q, p):
        source = below.at[q, z * PIECES + p]
        return rcopy(source, column_at(q, p, me), kf_sem.at[q, p, 0], kr_sem.at[q, me, p], space=partner)

    def column_own(q, p):
        return pltpu.make_async_copy(below.at[q, z * PIECES + p], column_at(q, p, me), ko_sem.at[q, p])

    def column_forward(q, p, j, d):
        at = column_at(q, p, j)
        return rcopy(at, at, kf_sem.at[q, p, d], kr_sem.at[q, j, p], space=partner)

    def columns_start(q, p):
        for d in reversed(range(1, pairs)):
            column_copy(q, p, d).start()
        column_pair(q, p).start()
        column_own(q, p).start()

    def columns_relay(q):
        @pl.loop(0, PIECES)
        def _(n):
            p = jnp.where(2 * z < time_count, PIECES - 1 - n, n)
            p = jnp.where((z == 0) | (z == last), PIECES - 1 - p, p)
            for d in range(1, pairs):
                column_forward(q, p, peer(d), d).wait_recv()
                column_forward(q, p, peer(d), d).start()

    def columns_finish(q):
        @pl.loop(0, PIECES)
        def _(p):
            for d in range(pairs):
                column_forward(q, p, peer(d) + 1 - 2 * core, d).wait_recv()
            for d in range(1, pairs):
                column_copy(q, p, d).wait_send()
                column_forward(q, p, peer(d), d).wait_send()
            column_pair(q, p).wait_send()
            column_own(q, p).wait()

    def finish_block(q, m):
        below[q, m] = (partial[q, m] + below[q, m].astype(F32) + above[q, m].astype(F32)).astype(BF16)
        row_copy(q, m).start()

        @pl.when((lax.div(m, PIECES) == z) & (q == streams - 1))
        def _():
            columns_start(q, lax.rem(m, PIECES))

    def up_step(n):
        at = n - LAG * z

        @pl.when((at >= 0) & (at < total))
        def _():
            q = lax.div(at, blocks)
            m = blocks - 1 - lax.rem(at, blocks)

            @pl.when(z > 0)
            def _():
                up_copy(at, q, m).wait_recv()

            @pl.when(z < last)
            def _():
                @pl.when(at >= RING)
                def _():
                    up_copy(at, q, m).wait_send()

                @pl.when(z == 0)
                def _():
                    up_out[lax.rem(at, RING)] = partial[q, m].astype(BF16)

                @pl.when(z > 0)
                def _():
                    up_out[lax.rem(at, RING)] = (partial[q, m] + below[q, m].astype(F32)).astype(BF16)

                up_copy(at, q, m).start()

            @pl.when((z == last) | ((z > 0) & (q * blocks + m + LAG * (last - z) < n)))
            def _():
                finish_block(q, m)

    def down_step(n):
        at = n - LAG * (last - z)

        @pl.when((at >= 0) & (at < total))
        def _():
            q = lax.div(at, blocks)
            m = lax.rem(at, blocks)

            @pl.when(z < last)
            def _():
                down_copy(at, q, m).wait_recv()

            @pl.when(z > 0)
            def _():
                @pl.when(at >= RING)
                def _():
                    down_copy(at, q, m).wait_send()

                @pl.when(z == last)
                def _():
                    down_out[lax.rem(at, RING)] = partial[q, m].astype(BF16)

                @pl.when(z < last)
                def _():
                    down_out[lax.rem(at, RING)] = (partial[q, m] + above[q, m].astype(F32)).astype(BF16)

                down_copy(at, q, m).start()

            @pl.when((z == 0) | ((z < last) & (q * blocks + blocks - 1 - m + LAG * z <= n)))
            def _():
                finish_block(q, m)

    for load in loads:
        load.wait()
    line_start(x_of(0))
    load_basis.start()
    load_tbasis.wait()
    line_start(t_line)
    t_share_step(0)
    load_basis.wait()
    spectral(0, z)
    work = [functools.partial(spectral, q, z) for q in range(1, reps)]
    for k in range(1, time_count):
        for p in range(PARTS):
            if work and k > 1:
                work.pop(0)()
            if p == 0 and k == max(1, time_count - 1):
                for q in range(1, reps):
                    line_start(x_of(q))
            line_part(x_of(0), k, p)
            if p == PARTS - 1:
                line_step(t_line, k)
                t_share_step(k)
            if work and k == 1:
                work.pop(0)()
        while work:
            work.pop(0)()
        work = [functools.partial(spectral_side, 0, k, side) for side in range(2)]
    while work:
        work.pop(0)()
    for q in range(reps - 1):
        if q == 0:
            t_share_each(lambda copy: copy.wait_recv())
        v = q * HALVES
        scale_own(q)
        gather_start(v)
        line_step(x_of(q + 1), 1)
        spectral_step(q + 1, 1, False)
        gather_near(v)
        for h in range(1, HALVES):
            gather_start(v + h)

        @pl.when((z > 0) & (z < last))
        def _():
            for k in range(2, time_count - 1):
                line_step(x_of(q + 1), k)
                spectral_step(q + 1, k, False)

        gather_far(v)

    after = {}

    def then(n, act, *args):
        after.setdefault(n, []).append(functools.partial(act, *args))

    def slices_flush(q):
        spectral_flush(q, 1)

        @pl.when((z > 0) & (z < last))
        def _():
            for k in range(2, time_count - 1):
                spectral_flush(q, k)

    def slices_of_ends(q):
        @pl.when((z == 0) | (z == last))
        def _():
            for k in range(2, time_count - 1):
                line_step(x_of(q), k)
                spectral_step(q, k)

    def columns_bulk(v):
        @pl.loop(0, PIECES)
        def _(p):
            columns_start(v, p)

    unit = max(PIECES // 2, 1)
    for q in range(reps):
        first = q * HALVES * blocks
        if q + 1 < reps:
            then(first + blocks - 5 * unit, gather_near, q * HALVES + 1)
            then(first + blocks - 5 * unit, slices_flush, q + 1)
            then(first + blocks - 4 * unit, slices_of_ends, q + 1)
            for k in range(max(2, time_count - 1), time_count):
                then(first + blocks - 2 * unit, line_step, x_of(q + 1), k)
                then(first + blocks - 2 * unit, spectral_step, q + 1, k)
        if q > 0:
            then(first - blocks + 3 * unit, scale_own, q)
            then(first - blocks + 3 * unit, gather_start, q * HALVES)
            then(first - 3 * unit, gather_near, q * HALVES)
            then(first - 1, gather_far, q * HALVES)
        for h in range(1, HALVES):
            v = q * HALVES + h
            if q > 0:
                then(first - 3 * unit, gather_start, v)
            if q > 0:
                then(v * blocks - 6 * unit, gather_near, v)
            then(v * blocks - 3 * unit, gather_far, v)
    for v in range(streams - 1):
        then(max((streams - 1) * blocks - 3 * unit, (v + 1) * blocks), columns_bulk, v)
    for v in range(streams - 1):
        then(total - 1 if v < streams - 2 else total + LAG * last - 2 * unit, columns_relay, v)

    def lines_drain():
        for q in range(reps):
            line_drain(x_of(q))
        line_drain(t_line)
        t_share_each(lambda copy: copy.wait_send())

        @pl.loop(0, time_count)
        def _(j):
            for d in range(pairs):
                pair_copy(reps - 1, j, d).wait_send()
                if d > 0:
                    chip_copy(reps - 1, j, d).wait_send()

    def rows_drain(begin, end):
        @pl.loop(begin, end)
        def _(n):
            row_copy(lax.div(n, blocks), lax.rem(n, blocks)).wait()

    then(total, lines_drain)
    for v in range(streams):
        then(total + 1, gather_drain, v)
    then(total + 1, rows_drain, 0, (streams - 1) * blocks)
    for v in range(streams - 2):
        then(min(total + 2, total + LAG * last - 1), columns_finish, v)

    @pl.loop(0, total + LAG * last)
    def _(n):
        v = lax.div(n, blocks)
        i = lax.rem(n, blocks)

        @pl.when((v < streams) & (i < time_count))
        def _():
            @pl.when(i == 0)
            def _():
                gather_finish(v)

            back(v, i)

        up_step(n)
        down_step(n)
        for at, acts in after.items():
            @pl.when(n == at)
            def _():
                for act in acts:
                    act()

    columns_relay(streams - 1)
    for v in range(max(streams - 2, 0), streams):
        columns_finish(v)
    rows_drain((streams - 1) * blocks, total)

    for n in range(total - min(RING, total), total):
        q, m = n // blocks, n % blocks

        @pl.when(z < last)
        def _():
            up_copy(n, q, m).wait_send()

        @pl.when(z > 0)
        def _():
            down_copy(n, q, m).wait_send()


def solve_field(series, basis, tbasis, time_eig, space_eig, space_count, time_count):
    reps, time_local, rows = series.shape
    depth = basis.shape[1]
    times = tbasis.shape[1]
    own = depth // space_count
    pairs = space_count // 2
    blocks = PIECES * time_count
    block_rows = rows // blocks
    streams = reps * HALVES
    width = times // HALVES
    dma = pltpu.SemaphoreType.DMA
    hbm = pl.BlockSpec(memory_space=pl.ANY)
    vmem = pl.BlockSpec(memory_space=pltpu.VMEM)
    return pl.pallas_call(
        functools.partial(field_kernel, space_count, time_count),
        out_shape=(
            jax.ShapeDtypeStruct((blocks, block_rows, reps * times), BF16),
            jax.ShapeDtypeStruct((space_count, PIECES, block_rows, reps * times), BF16),
        ),
        in_specs=[hbm, hbm, hbm, vmem, vmem],
        out_specs=(hbm, hbm),
        scratch_shapes=[
            pltpu.VMEM((rows, depth), BF16),
            pltpu.VMEM((reps, time_count, time_local, rows), BF16),
            pltpu.VMEM((time_count, time_local, times), BF16),
            pltpu.VMEM((pairs, time_count, time_local, own), BF16),
            pltpu.VMEM((reps, pairs, time_count, time_local, own), BF16),
            pltpu.VMEM((pairs - 1, time_count, time_local, own), BF16),
            pltpu.VMEM((reps, pairs - 1, time_count, time_local, own), BF16),
            pltpu.VMEM((reps, time_count, time_local, own), F32),
            pltpu.VMEM((streams, width, depth), BF16),
            pltpu.VMEM((streams, blocks, block_rows, width), F32),
            pltpu.VMEM((streams, blocks, block_rows, width), BF16),
            pltpu.VMEM((streams, blocks, block_rows, width), BF16),
            pltpu.VMEM((RING, block_rows, width), BF16),
            pltpu.VMEM((RING, block_rows, width), BF16),
            dma((2 + reps,)),
            dma((reps, 2, time_count, PARTS)),
            dma((reps, time_count, PARTS)),
            dma((2, time_count)),
            dma((time_count,)),
            dma((2, pairs, time_count)),
            dma((pairs, time_count)),
            dma((reps, pairs, time_count)),
            dma((pairs - 1, time_count)),
            dma((reps, pairs - 1, time_count)),
            dma((streams, pairs - 1, 2)),
            dma((streams, space_count, 2)),
            dma((streams, pairs, 2)),
            dma((RING,)),
            dma((streams * blocks,)),
            dma((RING,)),
            dma((streams * blocks,)),
            dma((streams * blocks,)),
            dma((streams, PIECES, pairs)),
            dma((streams, space_count, PIECES)),
            dma((streams, PIECES, pairs)),
            dma((streams, PIECES)),
        ],
        compiler_params=pltpu.CompilerParams(
            collective_id=0, has_side_effects=True, vmem_limit_bytes=VMEM_BYTES
        ),
    )(series, basis, tbasis, time_eig, space_eig)


def grad_kernel(reps, wide, rows, columns, eig_ref, basis_ref, alpha_ref, grad_ref, alpha_scr, weighted, *halves):
    tile, blocks, sub = grad_ref.shape
    depth = rows.shape[1]
    times = depth // reps
    for q in range(reps):
        at = slice(q * times, (q + 1) * times)
        weighted[:, at] = (rows[:, at].astype(F32) * eig_ref[...] / depth).astype(BF16)
        alpha_scr[pl.ds(q, tile, stride=reps), :] = lax.dot_general(
            rows[:, at], basis_ref[...], CONTRACT_LAST, preferred_element_type=F32
        )
    alpha_ref[...] = alpha_scr[...].astype(BF16).reshape(alpha_ref.shape)
    for w in range(0, sub, wide):
        half = halves[w // wide % 2]
        for a in range(blocks):
            part = lax.dot_general(
                weighted[...], columns[a, w : w + wide, :], CONTRACT_LAST, preferred_element_type=F32
            )
            for v in range(0, wide, 128):
                half[v // 128, pl.ds(a, tile, stride=blocks), :] = part[:, v : v + 128]
        for v in range(0, wide, 128):
            grad_ref[:, :, w + v : w + v + 128] = half[v // 128].astype(BF16).reshape(tile, blocks, 128)


def grad_and_alpha(rows, columns, time_eig, time_basis, reps):
    row_count, depth = rows.shape
    blocks, sub, _ = columns.shape
    time_local, times = time_basis.shape
    tile = min(row_count, 256)
    wide = min(sub, 256)
    return pl.pallas_call(
        functools.partial(grad_kernel, reps, wide),
        out_shape=(
            jax.ShapeDtypeStruct((row_count, reps, time_local), BF16),
            jax.ShapeDtypeStruct((row_count, blocks, sub), BF16),
        ),
        grid=(row_count // tile,),
        in_specs=[
            pl.BlockSpec((tile, depth), lambda i: (i, 0)),
            pl.BlockSpec((blocks, sub, depth), lambda i: (0, 0, 0)),
            pl.BlockSpec((1, times), lambda i: (0, 0)),
            pl.BlockSpec((time_local, times), lambda i: (0, 0)),
        ],
        out_specs=(
            pl.BlockSpec((tile, reps, time_local), lambda i: (i, 0, 0)),
            pl.BlockSpec((tile, blocks, sub), lambda i: (i, 0, 0)),
        ),
        scratch_shapes=[
            pltpu.VMEM((tile * reps, time_local), F32),
            pltpu.VMEM((tile, depth), BF16),
            pltpu.VMEM((wide // 128, tile * blocks, 128), F32),
            pltpu.VMEM((wide // 128, tile * blocks, 128), F32),
        ],
    )(rows, columns, time_eig[None, :], time_basis)


def per_device(series, space_basis, time_basis, space_eig, time_eig):
    space_count = lax.axis_size("space")
    time_count = lax.axis_size("tm")
    rows, columns = solve_field(
        jnp.transpose(series, (1, 2, 0)),
        space_basis,
        time_basis,
        time_eig[None, :],
        space_eig[None, :],
        space_count,
        time_count,
    )
    depth = rows.shape[-1]
    return grad_and_alpha(
        rows.reshape(-1, depth), columns.reshape(space_count, -1, depth), time_eig, time_basis, series.shape[1]
    )


def solution(mesh):
    return jax.shard_map(
        per_device,
        mesh=mesh,
        in_specs=(P("space", None, "tm"), P("space", "tm"), P("tm", None), P(), P()),
        out_specs=(P("space", None, "tm"), P("space", None, "tm")),
        check_vma=False,
    )
```
